32 devices in a mesh: groups: 2 (over y), strip: 8 (over z, x), chan: 2 (over core).
Axes of the slice: x: 2, y: 2, z: 4, core: 2. Of those that a mesh axis runs over, the one named last changes fastest.
Arguments:
- sky_cube: bfloat16 [32, 512, 1024], P('chan', 'strip', 'groups'), parts along dimension 2, may hold values from -80 to 80
- chan_flags: int32 [32], P('chan'), may hold values 0 or 1
Outputs:
- snr_peak: bfloat16 [32, 512, 1024], P('chan', 'strip', 'groups'), parts along dimension 2
The draws below stay inside these ranges and needn't reach their ends.
There are 2 independent parts, one for each index of `groups`. The reference program is written for one: setup_inputs(seed, part) draws one part's arguments, and reference() takes and returns one part's arrays. A program takes and returns all parts, laid end to end along the dimension named above; an argument that names none is the same for every part. Nothing has to cross between parts.
All inputs are finite; a program needn't handle non-finite values. No bound on the sum of `chan_flags` on one device may be relied on, other than what follows from the above.
Results may differ from the reference program's by a relative error of at most 0.0054.
Values may be sent and summed in bfloat16 or wider, within the bound.
No kernel may reach another device: no remote copies, remote signals or barrier semaphores. Data moves between devices by JAX's collectives and lax.ppermute only.
A program may use at most 64 MiB of HBM per device.

```python
import math
from functools import partial
import jax
import jax.numpy as jnp
import numpy as np
from jax import lax

COLS = 512
CHANNELS = 32
NROWS = 512


def draw_sky_cube(key, part):
    key_base, key_rows, key_cols, key_chan = jax.random.split(key, 4)
    grid_shape = (CHANNELS, NROWS, COLS)
    row_position = jnp.arange(NROWS, dtype=jnp.float32) / max(NROWS - 1, 1)
    row_trend = jnp.exp(row_position * math.log(3.0))
    base_noise = jax.random.truncated_normal(key_base, -6.0, 6.0, grid_shape, jnp.float32)
    row_scale = jnp.exp(jax.random.uniform(key_rows, (NROWS,), jnp.float32) * math.log(10.0))
    col_scale = jnp.exp(jax.random.uniform(key_cols, (COLS,), jnp.float32) * math.log(10.0))
    chan_scale = jnp.exp(jax.random.uniform(key_chan, (CHANNELS,), jnp.float32) * math.log(4.0))
    scaling = chan_scale[:, None, None] * (row_scale * row_trend)[None, :, None] * col_scale[None, None, :] * 0.01
    return (base_noise * scaling).astype(jnp.bfloat16)


def place_ends(result, stream_key, smallest, top_value):
    place = [jax.random.randint(jax.random.fold_in(stream_key, axis), (), 0, length) for axis, length in enumerate(result.shape)]
    main_axis = result.shape.index(max(result.shape))
    neighbour = place[:main_axis] + [(place[main_axis] + 1) % result.shape[main_axis]] + place[main_axis + 1:]
    return result.at[tuple(place)].set(smallest).at[tuple(neighbour)].set(top_value)


def setup_inputs(seed: int = 0, part: int = 0) -> dict:
    splits = jax.random.split(jax.random.key(seed), 3)
    own_keys = jax.random.split(jax.random.fold_in(splits[2], part), 3)
    sky_cube = draw_sky_cube(jax.random.fold_in(jax.random.fold_in(splits[2], part), 71), part)
    chan_flags = place_ends((jax.random.randint(splits[1], (CHANNELS,), 0, 8) < 1).astype(jnp.int32), jax.random.fold_in(splits[1], 1), 0, 1)
    return dict(sky_cube=sky_cube, chan_flags=chan_flags)


boxcar_widths = (3, 7)
gauss_settings = ((5.0, 8), (10.0, 15))
epsilon = 1e-06
clip_level = 3.0

def gauss_weights(fwhm, radius):
    offsets = np.arange(-15, 16)
    spread = fwhm / (2.0 * math.sqrt(2.0 * math.log(2.0)))
    weights = np.exp(-offsets ** 2 / (2.0 * spread ** 2)) * (np.abs(offsets) <= radius)
    weights = weights / weights.sum()
    return weights.astype(np.float32)

def spectral_mean(padded, box_width, chan_count):
    half_width = box_width // 2
    running = jnp.zeros((chan_count,) + padded.shape[1:], jnp.float32)
    for offset in range(-half_width, half_width + 1):
        running = running + padded[3 + offset:3 + offset + chan_count].astype(jnp.float32)
    return (running / box_width).astype(jnp.bfloat16)

def convolve(values, tap_values, along):
    size_along = values.shape[along]
    pad_spec = [(0, 0), (0, 0)]
    pad_spec[along] = (15, 15)
    padded = jnp.pad(values, pad_spec)
    running = jnp.zeros_like(values)
    for offset in range(31):
        running = running + tap_values[offset] * lax.slice_in_dim(padded, offset, offset + size_along, axis=along)
    return running

def smooth_plane(channel_plane, tap_values):
    rowwise = convolve(channel_plane.astype(jnp.float32), tap_values, 0).astype(jnp.bfloat16)
    return convolve(rowwise.astype(jnp.float32), tap_values, 1)

def noise_level(smoothed):
    pixels = smoothed.shape[1] * smoothed.shape[2]
    squares = smoothed * smoothed
    rough_sigma = jnp.sqrt(lax.optimization_barrier(jnp.sum(squares, axis=(1, 2))) / pixels + epsilon)
    clip_limit = (clip_level * rough_sigma) ** 2
    clipped = lax.optimization_barrier(jnp.sum(jnp.minimum(squares, clip_limit[:, None, None]), axis=(1, 2)))
    return jnp.sqrt(clipped / pixels + epsilon)

def reference(sky_cube, chan_flags):
    keep_mask = (1 - chan_flags).astype(jnp.bfloat16)
    masked = sky_cube * keep_mask[:, None, None]
    padded = jnp.pad(masked, ((3, 3), (0, 0), (0, 0)))
    chan_count = sky_cube.shape[0]
    tap_sets = [jnp.asarray(gauss_weights(fwhm, radius)).astype(jnp.bfloat16).astype(jnp.float32) for fwhm, radius in gauss_settings]
    peak_ratio = None
    for box_width in boxcar_widths:
        spectral = spectral_mean(padded, box_width, chan_count)
        kernels = [spectral.astype(jnp.float32)]
        for tap_values in tap_sets:
            kernels.append(lax.map(partial(smooth_plane, tap_values=tap_values), spectral))
        for smoothed in kernels:
            ratio_now = smoothed / noise_level(smoothed)[:, None, None]
            peak_ratio = ratio_now if peak_ratio is None else jnp.maximum(peak_ratio, ratio_now)
    return (peak_ratio * keep_mask.astype(jnp.float32)[:, None, None]).astype(jnp.bfloat16)
```

```python
import functools
import math

import jax
import jax.numpy as jnp
import numpy as np
from jax import lax
from jax.experimental import pallas as pl
from jax.experimental.pallas import tpu as pltpu
from jax.sharding import PartitionSpec as P

boxcar_widths = (3, 7)
gauss_settings = ((5.0, 8), (10.0, 15))
epsilon = 1e-06
clip_level = 3.0
RIM = 3
REACH = 15
EDGE = 16
LANES = 128
VMEM = pltpu.VMEM
SMEM = pltpu.SMEM


def gauss_weights(fwhm, radius):
    offsets = np.arange(-REACH, REACH + 1)
    spread = fwhm / (2.0 * math.sqrt(2.0 * math.log(2.0)))
    weights = np.exp(-(offsets**2) / (2.0 * spread**2)) * (np.abs(offsets) <= radius)
    weights = weights / weights.sum()
    return weights.astype(np.float32)


def band(out_positions, in_positions):
    offset = np.asarray(in_positions)[None, :] - np.asarray(out_positions)[:, None]
    inside = np.abs(offset) <= REACH
    index = np.clip(offset + REACH, 0, 2 * REACH)
    return np.stack([np.where(inside, gauss_weights(*s)[index], 0.0) for s in gauss_settings])


def constant(matrix):
    return jnp.asarray(matrix.astype(np.float32)).astype(jnp.bfloat16)


def square_sum(values):
    rows, cols = values.shape
    return fold(values * values)


def fold(values):
    rows, cols = values.shape
    total = None
    for r in range(0, rows, 8):
        for c in range(0, cols, LANES):
            part = values[r : r + 8, c : c + LANES]
            total = part if total is None else total + part
    return total


def spectral_tiles(load, store, chan_count):
    x = [load(c) for c in range(-RIM, chan_count + RIM)]
    for c in range(chan_count):
        s3 = x[c + 2] + x[c + 3] + x[c + 4]
        s7 = (x[c] + x[c + 1]) + s3 + (x[c + 5] + x[c + 6])
        store(0, c, (s3 * (1.0 / 3.0)).astype(jnp.bfloat16))
        store(1, c, (s7 * (1.0 / 7.0)).astype(jnp.bfloat16))


def column_pass(rows_ref, matrix_ref, out_ref, acc_ref, chan_count, block):
    per = rows_ref.shape[1] // (2 * chan_count)
    step = per * block
    for f in range(2):

        @pl.loop(0, 2 * chan_count // block)
        def _(m):
            start = pl.multiple_of(m * step, step)
            result = jnp.dot(
                rows_ref[f, pl.ds(start, step), :], matrix_ref[f], preferred_element_type=jnp.float32
            )
            out_ref[f, pl.ds(start, step), :] = result
            for i in range(block):
                slot = m * block + i
                k = lax.div(slot, chan_count) * 3 + 1 + f
                acc_ref[k * chan_count + lax.rem(slot, chan_count)] = square_sum(
                    result[i * per : (i + 1) * per]
                )


def middle_kernel(flags, sides, sky, rim, row_band, col_band, spec, smooth, sums, rowwise, acc):
    chan_count, n_rows, n_cols = sky.shape
    keep = [(1 - flags[c]).astype(jnp.float32) for c in range(chan_count)]
    side = [sides[i].astype(jnp.float32) for i in range(2)]

    @pl.loop(0, n_rows // 16)
    def _(t):
        rows = pl.ds(pl.multiple_of(t * 16, 16), 16)
        for lane in range(0, n_cols, LANES):
            cols = slice(lane, lane + LANES)

            def load(c):
                if c < 0:
                    return rim[0, c + RIM, rows, cols].astype(jnp.float32) * side[0]
                if c >= chan_count:
                    return rim[rim.shape[0] - 1, c - chan_count, rows, cols].astype(jnp.float32) * side[1]
                return sky[c, rows, cols].astype(jnp.float32) * keep[c]

            def store(w, c, value):
                spec[w, c, rows, cols] = value

            spectral_tiles(load, store, chan_count)

    per = rowwise.shape[1] // (2 * chan_count)

    @pl.loop(0, chan_count)
    def _(c):
        for w in range(2):
            plane = spec[w, c]
            acc[w * 3 * chan_count + c] = square_sum(plane.astype(jnp.float32))
            row = jnp.dot(row_band[...], plane, preferred_element_type=jnp.float32).astype(jnp.bfloat16)
            start = pl.multiple_of((w * chan_count + c) * per, per)
            for f in range(2):
                rowwise[f, pl.ds(start, per), :] = row[f * per : (f + 1) * per]

    column_pass(rowwise, col_band, smooth, acc, chan_count, 4)
    sums[...] = jnp.sum(acc[...], axis=1)


def share(acc_sum, peers):
    rows = acc_sum.shape[0]
    if rows < LANES:
        acc_sum = jnp.concatenate([acc_sum, jnp.zeros((LANES - rows, LANES), jnp.float32)], axis=0)
    total = jnp.sum(acc_sum.T, axis=0, keepdims=True)
    return jnp.broadcast_to(total, (peers, LANES))


def spread(shared):
    total = jnp.sum(shared, axis=0, keepdims=True)
    return jnp.broadcast_to(total, (LANES, LANES)).T


def edge_kernel(
    flags, sides, above, below, corner_above, corner_below, spec, row_band, col_band, sums, smooth, shared, rowwise, acc, frame
):
    chan_count, edge, n_cols = above.shape
    n_rows = spec.shape[2]
    keep = [(1 - flags[c]).astype(jnp.float32) for c in range(chan_count)]
    side = [sides[i].astype(jnp.float32) for i in range(2)]
    for strip, corner, base in ((above, corner_above, 0), (below, corner_below, edge + n_rows)):
        for lane in range(0, n_cols, LANES):
            cols = slice(lane, lane + LANES)

            def load(c):
                if c < 0:
                    return corner[0, c + RIM, :, cols].astype(jnp.float32) * side[0]
                if c >= chan_count:
                    return corner[corner.shape[0] - 1, c - chan_count, :, cols].astype(jnp.float32) * side[1]
                return strip[c, :, cols].astype(jnp.float32) * keep[c]

            def store(w, c, value):
                frame[w, c, base : base + edge, cols] = value

            spectral_tiles(load, store, chan_count)
    frame[:, :, edge : edge + n_rows, :] = spec[...]
    per = rowwise.shape[1] // (2 * chan_count)

    @pl.loop(0, chan_count)
    def _(c):
        for w in range(2):
            row = jnp.dot(row_band[...], frame[w, c], preferred_element_type=jnp.float32).astype(jnp.bfloat16)
            start = pl.multiple_of((w * chan_count + c) * per, per)
            for f in range(2):
                rowwise[f, pl.ds(start, per), :] = row[f * per : (f + 1) * per]

    acc[...] = jnp.zeros_like(acc)
    column_pass(rowwise, col_band, smooth, acc, chan_count, 4)
    shared[...] = share(sums[...] + jnp.sum(acc[...], axis=1), shared.shape[0])


def clip_kernel(pixels, shared_in, spec, middle, edges, shared, limit, acc):
    chan_count = spec.shape[1]
    rough = jnp.sqrt(spread(shared_in[...]) / pixels + epsilon)
    limit[...] = (clip_level * rough) ** 2
    per = middle.shape[1] // (2 * chan_count)

    @pl.loop(0, chan_count)
    def _(c):
        for w in range(2):
            start = pl.multiple_of((w * chan_count + c) * per, per)
            for f in range(-1, 2):
                slot = (w * 3 + 1 + f) * chan_count + c
                top = jnp.broadcast_to(limit[pl.ds(slot, 1), :], (8, LANES))
                total = None
                if f < 0:
                    parts = [spec[w, c].astype(jnp.float32)]
                else:
                    parts = [middle[f, pl.ds(start, per), :], edges[f, pl.ds(start, per), :]]
                for part in parts:
                    for r in range(0, part.shape[0], 8):
                        for l in range(0, part.shape[1], LANES):
                            value = part[r : r + 8, l : l + LANES]
                            value = jnp.minimum(value * value, top)
                            total = value if total is None else total + value
                acc[slot] = total

    shared[...] = share(jnp.sum(acc[...], axis=1), shared.shape[0])


def ratio_kernel(pixels, flags, shared_in, spec, middle, edges, out, scale):
    chan_count, n_rows, n_cols = out.shape
    edge = EDGE
    scale[...] = 1.0 / jnp.sqrt(spread(shared_in[...]) / pixels + epsilon)
    per = middle.shape[1] // (2 * chan_count)

    @pl.loop(0, chan_count)
    def _(c):
        keep = (1 - flags[c]).astype(jnp.float32)
        factors = [
            jnp.broadcast_to(scale[pl.ds(k * chan_count + c, 1), :], (16, LANES)) for k in range(6)
        ]
        for r in range(0, n_rows, 16):
            if r < edge:
                source, offset = edges, r
            elif r < n_rows - edge:
                source, offset = middle, r - edge
            else:
                source, offset = edges, r - (n_rows - edge) + edge
            for l in range(0, n_cols, LANES):
                cols = slice(l, l + LANES)
                best = None
                for w in range(2):
                    values = [spec[w, c, r : r + 16, cols].astype(jnp.float32)]
                    start = pl.multiple_of((w * chan_count + c) * per, per) + offset
                    start = pl.multiple_of(start, 16)
                    values += [source[f, pl.ds(start, 16), cols] for f in range(2)]
                    for f in range(3):
                        value = values[f] * factors[w * 3 + f]
                        best = value if best is None else jnp.maximum(best, value)
                out[c, r : r + 16, cols] = (best * keep).astype(jnp.bfloat16)


def specs(*spaces):
    return [pl.BlockSpec(memory_space=s) for s in spaces]


def shards(sky_cube, chan_flags):
    chan_count, n_rows, n_cols = sky_cube.shape
    strips, blocks = lax.axis_size("strip"), lax.axis_size("chan")
    pixels = n_rows * strips * n_cols
    keep_mask = (1 - chan_flags).astype(jnp.bfloat16)
    block = lax.axis_index("chan")

    down = [(i, i + 1) for i in range(strips - 1)]
    up = [(j, i) for i, j in down]
    above = lax.ppermute(sky_cube[:, n_rows - EDGE :], "strip", down)
    below = lax.ppermute(sky_cube[:, :EDGE], "strip", up)

    last = sky_cube[chan_count - RIM :] * keep_mask[chan_count - RIM :, None, None]
    first = sky_cube[:RIM] * keep_mask[:RIM, None, None]
    forth = [(i, i + 1) for i in range(blocks - 1)]
    back = [(j, i) for i, j in forth]
    if blocks == 2:
        moves = [(jnp.where(block == 0, last, first), forth + back)]
    else:
        moves = [(last, forth), (first, back)]
    rim, corner_above, corner_below = [], [], []
    for payload, pairs in moves:
        rim.append(lax.ppermute(payload, "chan", pairs))
        for rows, strip_pairs, into in (
            (payload[:, n_rows - EDGE :], down, corner_above),
            (payload[:, :EDGE], up, corner_below),
        ):
            both = [(s * blocks + a, t * blocks + b) for s, t in strip_pairs for a, b in pairs]
            into.append(lax.ppermute(rows, ("strip", "chan"), both))
    rim, corner_above, corner_below = (jnp.stack(v) for v in (rim, corner_above, corner_below))
    sides = jnp.stack([block > 0, block < blocks - 1]).astype(jnp.int32)

    mid = n_rows - 2 * EDGE
    own = np.arange(n_rows)
    mid_band = constant(band(own[EDGE : n_rows - EDGE], own).reshape(2 * mid, n_rows))
    edge_rows = np.concatenate([own[:EDGE], own[n_rows - EDGE :]])
    framed = np.arange(-EDGE, n_rows + EDGE)
    edge_band = constant(band(edge_rows, framed).reshape(4 * EDGE, n_rows + 2 * EDGE))
    cols = np.arange(n_cols)
    col_band = constant(band(cols, cols).transpose(0, 2, 1))

    f32, bf16 = jnp.float32, jnp.bfloat16
    slots = 6 * chan_count
    params = pltpu.CompilerParams(vmem_limit_bytes=32 * 2**20)

    def call(kernel, ins, outs, scratch, flops, name):
        return pl.pallas_call(
            kernel,
            in_specs=specs(*ins),
            out_specs=specs(*[VMEM] * len(outs)),
            out_shape=[jax.ShapeDtypeStruct(s, d) for s, d in outs],
            scratch_shapes=[VMEM(s, d) for s, d in scratch],
            compiler_params=params,
            cost_estimate=pl.CostEstimate(flops=flops, bytes_accessed=8 * 2**20, transcendentals=0),
            name=name,
        )

    spec, middle, sums = call(
        middle_kernel,
        [SMEM, SMEM] + [VMEM] * 4,
        [
            ((2, chan_count, n_rows, n_cols), bf16),
            ((2, 2 * chan_count * mid, n_cols), f32),
            ((slots, LANES), f32),
        ],
        [((2, 2 * chan_count * mid, n_cols), bf16), ((slots, 8, LANES), f32)],
        2 * 10**9,
        "middle_rows",
    )(chan_flags, sides, sky_cube, rim, mid_band, col_band)
    edges, shared = call(
        edge_kernel,
        [SMEM, SMEM] + [VMEM] * 8,
        [((2, 4 * chan_count * EDGE, n_cols), f32), ((strips, LANES), f32)],
        [
            ((2, 4 * chan_count * EDGE, n_cols), bf16),
            ((slots, 8, LANES), f32),
            ((2, chan_count, n_rows + 2 * EDGE, n_cols), bf16),
        ],
        2 * 10**9,
        "edge_rows",
    )(chan_flags, sides, above, below, corner_above, corner_below, spec, edge_band, col_band, sums)
    shared = lax.all_to_all(shared, "strip", 0, 0, tiled=True)
    (shared,) = call(
        functools.partial(clip_kernel, pixels),
        [VMEM] * 4,
        [((strips, LANES), f32)],
        [((LANES, LANES), f32), ((slots, 8, LANES), f32)],
        10**8,
        "clip",
    )(shared, spec, middle, edges)
    shared = lax.all_to_all(shared, "strip", 0, 0, tiled=True)
    (out,) = call(
        functools.partial(ratio_kernel, pixels),
        [SMEM] + [VMEM] * 4,
        [((chan_count, n_rows, n_cols), bf16)],
        [((LANES, LANES), f32)],
        10**8,
        "ratio",
    )(chan_flags, shared, spec, middle, edges)
    return out


def solution(mesh):
    in_specs = (P("chan", "strip", "groups"), P("chan"))
    out_specs = P("chan", "strip", "groups")
    return jax.shard_map(shards, mesh=mesh, in_specs=in_specs, out_specs=out_specs, check_vma=False)
```

```python
import functools
import math

import jax
import jax.numpy as jnp
import numpy as np
from jax import lax
from jax.experimental import pallas as pl
from jax.experimental.pallas import tpu as pltpu
from jax.sharding import PartitionSpec as P

gauss_settings = ((5.0, 8), (10.0, 15))
epsilon = 1e-06
clip_level = 3.0
RIM = 3
REACH = 15
EDGE = 16
LANES = 128
VMEM = pltpu.VMEM
SMEM = pltpu.SMEM


def gauss_weights(fwhm, radius):
    offsets = np.arange(-REACH, REACH + 1)
    spread = fwhm / (2.0 * math.sqrt(2.0 * math.log(2.0)))
    weights = np.exp(-(offsets**2) / (2.0 * spread**2)) * (np.abs(offsets) <= radius)
    weights = weights / weights.sum()
    return weights.astype(np.float32)


def band(out_positions, in_positions):
    offset = np.asarray(in_positions)[None, :] - np.asarray(out_positions)[:, None]
    inside = np.abs(offset) <= REACH
    index = np.clip(offset + REACH, 0, 2 * REACH)
    return np.stack([np.where(inside, gauss_weights(*s)[index], 0.0) for s in gauss_settings])


def constant(matrix):
    return jnp.asarray(matrix.astype(np.float32)).astype(jnp.bfloat16)


def fold(values):
    rows, cols = values.shape
    total = None
    for r in range(0, rows, 8):
        for c in range(0, cols, LANES):
            part = values[r : r + 8, c : c + LANES]
            total = part if total is None else total + part
    return total


def wide(ref, row, rows=EDGE):
    return jnp.broadcast_to(ref[pl.ds(row, 1), :], (rows, LANES))


def spectral_tiles(load, store, chan_count):
    x = [load(c) for c in range(-RIM, chan_count + RIM)]
    for c in range(chan_count):
        s3 = x[c + 2] + x[c + 3] + x[c + 4]
        s7 = (x[c] + x[c + 1]) + s3 + (x[c + 5] + x[c + 6])
        store(0, c, (s3 * (1.0 / 3.0)).astype(jnp.bfloat16))
        store(1, c, (s7 * (1.0 / 7.0)).astype(jnp.bfloat16))


def row_pass(band_ref, plane, rowwise, chan_count, group):
    per = rowwise.shape[1] // (2 * chan_count)

    @pl.loop(0, chan_count // group)
    def _(g):
        for i in range(group):
            c = g * group + i
            for w in range(2):
                row = jnp.dot(band_ref[...], plane(w, c), preferred_element_type=jnp.float32)
                row = row.astype(jnp.bfloat16)
                start = pl.multiple_of((w * chan_count + c) * per, per)
                for f in range(2):
                    rowwise[f, pl.ds(start, per), :] = row[f * per : (f + 1) * per]


def column_pass(rowwise, matrix, out, acc, chan_count):
    n_cols = out.shape[2]
    per = rowwise.shape[1] // (2 * chan_count)
    block = 2 * LANES
    half = LANES
    for f in range(2):
        diagonal = []
        for i, b in enumerate(range(0, n_cols, block)):
            x = rowwise[f, :, b : b + block]
            diagonal.append(jnp.dot(x, matrix[f, i], preferred_element_type=jnp.float32))
        seams = []
        for i, b in enumerate(range(half, n_cols - block, block)):
            x = rowwise[f, :, b : b + block]
            seams.append(
                jnp.dot(x, matrix[f, n_cols // block + i], preferred_element_type=jnp.float32)
            )
        for slot in range(2 * chan_count):
            rows = slice(slot * per, (slot + 1) * per)
            total = None
            for l in range(0, n_cols, LANES):
                b, right = l // block, l % block
                value = diagonal[b][rows, right : right + LANES]
                if right and b < len(seams):
                    value = value + seams[b][rows, :LANES]
                if not right and b > 0:
                    value = value + seams[b - 1][rows, LANES:]
                out[f, rows, l : l + LANES] = value
                part = fold(value * value)
                total = part if total is None else total + part
            w, c = slot // chan_count, slot % chan_count
            acc[(w * 3 + 1 + f) * chan_count + c] = total


def pick_kernel(sky, last_rows, first_rows, sems):
    n_rows = sky.shape[1]
    copies = [
        pltpu.make_async_copy(sky.at[:, n_rows - EDGE :, :], last_rows, sems.at[0]),
        pltpu.make_async_copy(sky.at[:, :EDGE, :], first_rows, sems.at[1]),
    ]
    for copy in copies:
        copy.start()
    for copy in copies:
        copy.wait()


def prepare_kernel(flags, sides, sky, band_in, matrix_in, own, band, matrix, rims, keep, flag, sems):
    chan_count, n_rows, _ = sky.shape
    copies = [
        pltpu.make_async_copy(flags, flag, sems.at[0]),
        pltpu.make_async_copy(sky, own, sems.at[1]),
        pltpu.make_async_copy(matrix_in, matrix, sems.at[2]),
        pltpu.make_async_copy(band_in, band, sems.at[3]),
    ]
    for copy in copies:
        copy.start()
    for copy in copies:
        copy.wait()
    keeps = [(1 - flag[c]).astype(jnp.float32) for c in range(chan_count)]
    for c in range(chan_count):
        keep[c : c + 1, :] = jnp.full((1, LANES), keeps[c], jnp.float32)
    for i in range(2):
        value = jnp.full((1, LANES), sides[i].astype(jnp.float32), jnp.float32)
        keep[chan_count + i : chan_count + i + 1, :] = value
    towards = sides[1].astype(jnp.float32)
    for i in range(RIM):
        tail, head = chan_count - RIM + i, i
        for r in range(0, n_rows, EDGE):
            rows = slice(r, r + EDGE)
            tails = own[tail, rows, :].astype(jnp.float32) * keeps[tail]
            heads = own[head, rows, :].astype(jnp.float32) * keeps[head]
            if rims.shape[0] == 1:
                rims[0, i, rows, :] = (heads + (tails - heads) * towards).astype(jnp.bfloat16)
            else:
                rims[0, i, rows, :] = tails.astype(jnp.bfloat16)
                rims[1, i, rows, :] = heads.astype(jnp.bfloat16)


def corner_kernel(keep, above, below, corners):
    chan_count, _, n_cols = above.shape
    for part, source in enumerate((above, below)):
        for i in range(RIM):
            tail, head = chan_count - RIM + i, i
            for l in range(0, n_cols, LANES):
                cols = slice(l, l + LANES)
                tails = source[tail, :, cols].astype(jnp.float32) * wide(keep, tail)
                heads = source[head, :, cols].astype(jnp.float32) * wide(keep, head)
                if corners.shape[0] == 1:
                    value = heads + (tails - heads) * wide(keep, chan_count + 1)
                    corners[0, part * RIM + i, :, cols] = value.astype(jnp.bfloat16)
                else:
                    corners[0, part * RIM + i, :, cols] = tails.astype(jnp.bfloat16)
                    corners[1, part * RIM + i, :, cols] = heads.astype(jnp.bfloat16)


def middle_kernel(keep, sky, rim, row_band, matrix, spec, smooth, sums, rowwise, acc):
    chan_count, n_rows, n_cols = sky.shape

    @pl.loop(0, n_rows // EDGE)
    def _(t):
        rows = pl.ds(pl.multiple_of(t * EDGE, EDGE), EDGE)
        for lane in range(0, n_cols, LANES):
            cols = slice(lane, lane + LANES)

            def load(c):
                if c < 0:
                    return rim[0, c + RIM, rows, cols].astype(jnp.float32) * wide(keep, chan_count)
                if c >= chan_count:
                    value = rim[rim.shape[0] - 1, c - chan_count, rows, cols].astype(jnp.float32)
                    return value * wide(keep, chan_count + 1)
                return sky[c, rows, cols].astype(jnp.float32) * wide(keep, c)

            def store(w, c, value):
                spec[w, c, rows, cols] = value

            spectral_tiles(load, store, chan_count)

    def plane(w, c):
        value = spec[w, c]
        wide_value = value.astype(jnp.float32)
        acc[w * 3 * chan_count + c] = fold(wide_value * wide_value)
        return value

    row_pass(row_band, plane, rowwise, chan_count, 4)
    column_pass(rowwise, matrix, smooth, acc, chan_count)
    sums[...] = jnp.sum(acc[...], axis=1)


def share(acc_sum, peers):
    rows = acc_sum.shape[0]
    if rows < LANES:
        acc_sum = jnp.concatenate([acc_sum, jnp.zeros((LANES - rows, LANES), jnp.float32)], axis=0)
    total = jnp.sum(acc_sum.T, axis=0, keepdims=True)
    return jnp.broadcast_to(total, (peers, LANES))


def spread(shared):
    total = jnp.sum(shared, axis=0, keepdims=True)
    return jnp.broadcast_to(total, (LANES, LANES)).T


def edge_kernel(
    keep, above, below, corners, spec, row_band, matrix, sums, smooth, shared, rowwise, acc, frame
):
    chan_count, edge, n_cols = above.shape
    n_rows = spec.shape[2]
    for strip, part, base in ((above, 0, 0), (below, RIM, edge + n_rows)):
        for lane in range(0, n_cols, LANES):
            cols = slice(lane, lane + LANES)

            def load(c):
                if c < 0:
                    return corners[0, part + c + RIM, :, cols].astype(jnp.float32) * wide(keep, chan_count)
                if c >= chan_count:
                    value = corners[corners.shape[0] - 1, part + c - chan_count, :, cols].astype(jnp.float32)
                    return value * wide(keep, chan_count + 1)
                return strip[c, :, cols].astype(jnp.float32) * wide(keep, c)

            def store(w, c, value):
                frame[w, c, base : base + edge, cols] = value

            spectral_tiles(load, store, chan_count)
    frame[:, :, edge : edge + n_rows, :] = spec[...]
    row_pass(row_band, lambda w, c: frame[w, c], rowwise, chan_count, 4)
    acc[...] = jnp.zeros_like(acc)
    column_pass(rowwise, matrix, smooth, acc, chan_count)
    shared[...] = share(sums[...] + jnp.sum(acc[...], axis=1), shared.shape[0])


def clip_kernel(pixels, shared_in, spec, middle, edges, shared, limit, acc):
    chan_count = spec.shape[1]
    rough = jnp.sqrt(spread(shared_in[...]) / pixels + epsilon)
    limit[...] = (clip_level * rough) ** 2
    per = middle.shape[1] // (2 * chan_count)

    @pl.loop(0, chan_count)
    def _(c):
        for w in range(2):
            start = pl.multiple_of((w * chan_count + c) * per, per)
            for f in range(-1, 2):
                slot = (w * 3 + 1 + f) * chan_count + c
                top = jnp.broadcast_to(limit[pl.ds(slot, 1), :], (8, LANES))
                total = None
                if f < 0:
                    parts = [spec[w, c].astype(jnp.float32)]
                else:
                    parts = [middle[f, pl.ds(start, per), :], edges[f, pl.ds(start, per), :]]
                for part in parts:
                    for r in range(0, part.shape[0], 8):
                        for l in range(0, part.shape[1], LANES):
                            value = part[r : r + 8, l : l + LANES]
                            value = jnp.minimum(value * value, top)
                            total = value if total is None else total + value
                acc[slot] = total

    shared[...] = share(jnp.sum(acc[...], axis=1), shared.shape[0])


def ratio_kernel(pixels, keep, shared_in, spec, middle, edges, out, scale, staged, sems):
    chan_count, n_rows, n_cols = out.shape
    edge = EDGE
    scale[...] = 1.0 / jnp.sqrt(spread(shared_in[...]) / pixels + epsilon)
    per = middle.shape[1] // (2 * chan_count)
    parts = sems.shape[0]
    group = chan_count // parts

    def channel(c):
        keep_tile = wide(keep, c)
        factors = [wide(scale, k * chan_count + c) for k in range(6)]
        for r in range(0, n_rows, 16):
            if r < edge:
                source, offset = edges, r
            elif r < n_rows - edge:
                source, offset = middle, r - edge
            else:
                source, offset = edges, r - (n_rows - edge) + edge
            for l in range(0, n_cols, LANES):
                cols = slice(l, l + LANES)
                best = None
                for w in range(2):
                    values = [spec[w, c, r : r + 16, cols].astype(jnp.float32)]
                    start = pl.multiple_of((w * chan_count + c) * per + offset, 16)
                    values += [source[f, pl.ds(start, 16), cols] for f in range(2)]
                    for f in range(3):
                        value = values[f] * factors[w * 3 + f]
                        best = value if best is None else jnp.maximum(best, value)
                staged[c, r : r + 16, cols] = (best * keep_tile).astype(jnp.bfloat16)

    copies = []
    for p in range(parts):
        pl.loop(p * group, (p + 1) * group)(channel)
        s = slice(p * group, (p + 1) * group)
        copies.append(pltpu.make_async_copy(staged.at[s], out.at[s], sems.at[p]))
        copies[-1].start()
    for copy in copies:
        copy.wait()


def specs(spaces):
    return [pl.BlockSpec(memory_space=s) for s in spaces]


def shards(sky_cube, chan_flags):
    chan_count, n_rows, n_cols = sky_cube.shape
    strips, blocks = lax.axis_size("strip"), lax.axis_size("chan")
    pixels = n_rows * strips * n_cols
    block = lax.axis_index("chan")
    f32, bf16 = jnp.float32, jnp.bfloat16
    slots = 6 * chan_count
    mid = n_rows - 2 * EDGE
    turns = 1 if blocks == 2 else 2

    def call(kernel, ins, outs, scratch, flops, out_spaces=None):
        return pl.pallas_call(
            kernel,
            in_specs=specs(ins),
            out_specs=specs(out_spaces or [VMEM] * len(outs)),
            out_shape=[jax.ShapeDtypeStruct(s, d) for s, d in outs],
            scratch_shapes=scratch,
            compiler_params=pltpu.CompilerParams(vmem_limit_bytes=32 * 2**20),
            cost_estimate=pl.CostEstimate(flops=flops, bytes_accessed=8 * 2**20, transcendentals=0),
        )

    own_rows = np.arange(n_rows)
    mid_band = constant(band(own_rows[EDGE : n_rows - EDGE], own_rows).reshape(2 * mid, n_rows))
    edge_rows = np.concatenate([own_rows[:EDGE], own_rows[n_rows - EDGE :]])
    framed = np.arange(-EDGE, n_rows + EDGE)
    edge_band = constant(band(edge_rows, framed).reshape(4 * EDGE, n_rows + 2 * EDGE))
    cols = np.arange(n_cols)
    matrix = band(cols, cols).transpose(0, 2, 1)
    side = 2 * LANES
    same = cols[:, None] // side == cols[None, :] // side
    starts = np.arange(0, n_cols, side)
    pieces = [(matrix * same)[:, b : b + side, b : b + side] for b in starts]
    pieces += [(matrix * ~same)[:, b : b + side, b : b + side] for b in starts[:-1] + LANES]
    matrix = constant(np.stack(pieces, axis=1))

    sky_cube = pltpu.with_memory_space_constraint(sky_cube, pltpu.HBM)
    chan_flags = pltpu.with_memory_space_constraint(chan_flags, pltpu.HBM)
    matrix = pltpu.with_memory_space_constraint(matrix, pltpu.HBM)
    mid_band = pltpu.with_memory_space_constraint(mid_band, pltpu.HBM)

    rows_block = ((chan_count, EDGE, n_cols), bf16)
    last_rows, first_rows = call(
        pick_kernel, [pltpu.HBM], [rows_block, rows_block], [pltpu.SemaphoreType.DMA((2,))], 10**6
    )(sky_cube)

    onward = [(i, i + 1) for i in range(strips - 1)]
    backward = [(j, i) for i, j in onward]
    above = lax.ppermute(last_rows, "strip", onward)
    below = lax.ppermute(first_rows, "strip", backward)

    sides = jnp.stack([block > 0, block < blocks - 1]).astype(jnp.int32)
    own, mid_band, matrix, rims, keep = call(
        prepare_kernel,
        [pltpu.HBM, SMEM, pltpu.HBM, pltpu.HBM, pltpu.HBM],
        [
            ((chan_count, n_rows, n_cols), bf16),
            (mid_band.shape, bf16),
            (matrix.shape, bf16),
            ((turns, RIM, n_rows, n_cols), bf16),
            ((chan_count + 8, LANES), f32),
        ],
        [SMEM((chan_count,), jnp.int32), pltpu.SemaphoreType.DMA((4,))],
        10**6,
    )(chan_flags, sides, sky_cube, mid_band, matrix)

    forth = [(i, i + 1) for i in range(blocks - 1)]
    back = [(j, i) for i, j in forth]
    moves = [forth + back] if blocks == 2 else [forth, back]

    def across(payload):
        sent = [lax.ppermute(payload[i : i + 1], "chan", p) for i, p in enumerate(moves)]
        return jnp.concatenate(sent)

    rim = across(rims)
    spec, middle, sums = call(
        middle_kernel,
        [VMEM] * 5,
        [
            ((2, chan_count, n_rows, n_cols), bf16),
            ((2, 2 * chan_count * mid, n_cols), f32),
            ((slots, LANES), f32),
        ],
        [VMEM((2, 2 * chan_count * mid, n_cols), bf16), VMEM((slots, 8, LANES), f32)],
        2 * 10**9,
    )(keep, own, rim, mid_band, matrix)

    (corners,) = call(
        corner_kernel, [VMEM] * 3, [((turns, 2 * RIM, EDGE, n_cols), bf16)], [], 10**6
    )(keep, above, below)
    corners = across(corners)

    edges, shared = call(
        edge_kernel,
        [VMEM] * 8,
        [((2, 4 * chan_count * EDGE, n_cols), f32), ((strips, LANES), f32)],
        [
            VMEM((2, 4 * chan_count * EDGE, n_cols), bf16),
            VMEM((slots, 8, LANES), f32),
            VMEM((2, chan_count, n_rows + 2 * EDGE, n_cols), bf16),
        ],
        2 * 10**9,
    )(keep, above, below, corners, spec, edge_band, matrix, sums)
    shared = lax.all_to_all(shared, "strip", 0, 0, tiled=True)
    (shared,) = call(
        functools.partial(clip_kernel, pixels),
        [VMEM] * 4,
        [((strips, LANES), f32)],
        [VMEM((LANES, LANES), f32), VMEM((slots, 8, LANES), f32)],
        10**8,
    )(shared, spec, middle, edges)
    shared = lax.all_to_all(shared, "strip", 0, 0, tiled=True)
    (out,) = call(
        functools.partial(ratio_kernel, pixels),
        [VMEM] * 5,
        [((chan_count, n_rows, n_cols), bf16)],
        [
            VMEM((LANES, LANES), f32),
            VMEM((chan_count, n_rows, n_cols), bf16),
            pltpu.SemaphoreType.DMA((4,)),
        ],
        10**8,
        [pltpu.HBM],
    )(keep, shared, spec, middle, edges)
    return out


def solution(mesh):
    in_specs = (P("chan", "strip", "groups"), P("chan"))
    out_specs = P("chan", "strip", "groups")
    return jax.shard_map(shards, mesh=mesh, in_specs=in_specs, out_specs=out_specs, check_vma=False)
```

```python
import functools
import math

import jax
import jax.numpy as jnp
import numpy as np
from jax import lax
from jax.experimental import pallas as pl
from jax.experimental.pallas import tpu as pltpu
from jax.sharding import PartitionSpec as P

gauss_settings = ((5.0, 8), (10.0, 15))
epsilon = 1e-06
clip_level = 3.0
RIM = 3
REACH = 15
EDGE = 16
LANES = 128
BLOCK = 2 * LANES
VMEM, HBM, SMEM = pltpu.VMEM, pltpu.HBM, pltpu.SMEM
f32, bf16 = jnp.float32, jnp.bfloat16


def gauss_weights(fwhm, radius):
    offsets = np.arange(-REACH, REACH + 1)
    spread = fwhm / (2.0 * math.sqrt(2.0 * math.log(2.0)))
    weights = np.exp(-(offsets**2) / (2.0 * spread**2)) * (np.abs(offsets) <= radius)
    weights = weights / weights.sum()
    return weights.astype(np.float32)


def band(out_positions, in_positions):
    offset = np.asarray(in_positions)[None, :] - np.asarray(out_positions)[:, None]
    inside = np.abs(offset) <= REACH
    index = np.clip(offset + REACH, 0, 2 * REACH)
    return np.stack([np.where(inside, gauss_weights(*s)[index], 0.0) for s in gauss_settings])


def constant(matrix):
    return jnp.asarray(matrix.astype(np.float32)).astype(bf16)


def fold(values):
    rows, cols = values.shape
    total = None
    for r in range(0, rows, 8):
        for c in range(0, cols, LANES):
            part = values[r : r + 8, c : c + LANES]
            total = part if total is None else total + part
    return total


def wide(ref, row, rows=EDGE):
    return jnp.broadcast_to(ref[pl.ds(row, 1), :], (rows, LANES))


def towards(chan_count, turns):
    last = chan_count - RIM
    if turns == 1:
        return [jnp.where(lax.axis_index("chan") == 0, last, 0)]
    return [last, 0]


def pair_rows(n_rows, pair):
    odd = lax.rem(lax.axis_index("strip"), 2)
    at_end = odd == pair
    return pl.multiple_of(jnp.where(at_end, n_rows - EDGE, 0), EDGE)


def spectral_slot(chan_count, w, c):
    return w * chan_count + c


def smooth_slot(chan_count, w, f, c):
    return (2 + 2 * w + f) * chan_count + c


def spectral_tiles(load, store, chan_count):
    x = [load(c) for c in range(-RIM, chan_count + RIM)]
    for c in range(chan_count):
        s3 = x[c + 2] + x[c + 3] + x[c + 4]
        s7 = (x[c] + x[c + 1]) + s3 + (x[c + 5] + x[c + 6])
        store(0, c, (s3 * (1.0 / 3.0)).astype(bf16))
        store(1, c, (s7 * (1.0 / 7.0)).astype(bf16))


def spectral_rows(keep, body, rim, store, chan_count, n_cols, rows):
    for lane in range(0, n_cols, LANES):
        cols = slice(lane, lane + LANES)

        def load(c):
            if c < 0:
                value, row = rim[0, c + RIM, rows, cols], chan_count
            elif c >= chan_count:
                value, row = rim[rim.shape[0] - 1, c - chan_count, rows, cols], chan_count + 1
            else:
                value, row = body[c, rows, cols], c
            return value.astype(f32) * wide(keep, row)

        spectral_tiles(load, functools.partial(store, cols), chan_count)


def row_pass(row_band, plane, rowwise, chan_count, group):
    per = rowwise.shape[1] // (2 * chan_count)

    @pl.loop(0, chan_count // group)
    def _(g):
        taps = row_band()
        for i in range(group):
            c = g * group + i
            for w in range(2):
                row = jnp.dot(taps, plane(w, c), preferred_element_type=f32).astype(bf16)
                start = pl.multiple_of((w * chan_count + c) * per, per)
                for f in range(2):
                    rowwise[f, pl.ds(start, per), :] = row[f * per : (f + 1) * per]


def column_pass(rowwise, matrix, out, add, chan_count):
    n_cols = out.shape[2]
    per = rowwise.shape[1] // (2 * chan_count)
    blocks = n_cols // BLOCK
    for f in range(2):
        products = []
        for i in range(2 * blocks - 1):
            b = i * BLOCK if i < blocks else (i - blocks) * BLOCK + LANES
            x = rowwise[f, :, b : b + BLOCK]
            products.append(jnp.dot(x, matrix[f, i], preferred_element_type=f32))
        diagonal, seams = products[:blocks], products[blocks:]
        for slot in range(2 * chan_count):
            rows = slice(slot * per, (slot + 1) * per)
            total = None
            for l in range(0, n_cols, LANES):
                b, right = l // BLOCK, l % BLOCK
                value = diagonal[b][rows, right : right + LANES]
                if right and b < len(seams):
                    value = value + seams[b][rows, :LANES]
                if not right and b > 0:
                    value = value + seams[b - 1][rows, LANES:]
                out[f, rows, l : l + LANES] = value
                part = fold(value * value)
                total = part if total is None else total + part
            add(slot // chan_count, f, slot % chan_count, total)


def run(copies):
    for copy in copies:
        copy.start()
    for copy in copies:
        copy.wait()


def pick_kernel(sky, first_pair, second_pair, sems):
    pieces = (first_pair, second_pair)
    rows = [pl.ds(pair_rows(sky.shape[1], pair), EDGE) for pair in range(2)]
    run(
        [
            pltpu.make_async_copy(sky.at[:, rows[pair], :], pieces[pair], sems.at[pair])
            for pair in range(2)
        ]
    )


def rim_kernel(flags, sky, rims, keep, flag, raw, sems):
    chan_count, _, _ = sky.shape
    turns = rims.shape[0]
    first = towards(chan_count, turns)
    copies = [pltpu.make_async_copy(flags, flag, sems.at[turns])]
    for turn in range(turns):
        source = sky.at[pl.ds(first[turn], RIM)]
        copies.append(pltpu.make_async_copy(source, raw.at[turn], sems.at[turn]))
    run(copies)
    for c in range(chan_count):
        keep[c : c + 1, :] = jnp.full((1, LANES), (1 - flag[c]).astype(f32), f32)
    block = lax.axis_index("chan")
    for i, inside in enumerate((block > 0, block < lax.axis_size("chan") - 1)):
        value = jnp.full((1, LANES), inside.astype(jnp.int32).astype(f32), f32)
        keep[chan_count + i : chan_count + i + 1, :] = value
    for turn in range(turns):
        for i in range(RIM):
            factor = (1 - flag[first[turn] + i]).astype(f32)
            rims[turn, i] = (raw[turn, i].astype(f32) * factor).astype(bf16)


def load_kernel(sky, mid_in, edge_in, matrix_in, own, mid_band, edge_band, matrix, sems):
    run(
        [
            pltpu.make_async_copy(sky, own, sems.at[0]),
            pltpu.make_async_copy(matrix_in, matrix, sems.at[1]),
            pltpu.make_async_copy(mid_in, mid_band, sems.at[2]),
            pltpu.make_async_copy(edge_in, edge_band, sems.at[3]),
        ]
    )


def corner_kernel(keep, halo, corners):
    chan_count, _, n_cols = halo.shape
    for turn, first in enumerate(towards(chan_count, corners.shape[0])):
        for i in range(RIM):
            factor = wide(keep, first + i)
            for l in range(0, n_cols, LANES):
                cols = slice(l, l + LANES)
                corners[turn, i, :, cols] = (halo[first + i, :, cols].astype(f32) * factor).astype(bf16)


def middle_kernel(keep, sky, rim, row_band, matrix, spec, smooth, sums, rowwise, acc):
    chan_count, n_rows, n_cols = sky.shape

    @pl.loop(0, n_rows // EDGE)
    def _(t):
        rows = pl.ds(pl.multiple_of(t * EDGE, EDGE), EDGE)

        def store(cols, w, c, value):
            spec[w, c, rows, cols] = value

        spectral_rows(keep, sky, rim, store, chan_count, n_cols, rows)

    def plane(w, c):
        value = spec[w, c]
        exact = value.astype(f32)
        acc[spectral_slot(chan_count, w, c)] = fold(exact * exact)
        return value

    def add(w, f, c, total):
        acc[smooth_slot(chan_count, w, f, c)] = total

    row_pass(lambda: row_band[...], plane, rowwise, chan_count, 4)
    column_pass(rowwise, matrix, smooth, add, chan_count)
    sums[...] = jnp.sum(acc[...], axis=1)


def edge_kernel(pair, keep, halo, corners, spec, row_band, matrix, sums, smooth, sums_out, rowwise, acc, frame):
    chan_count, n_rows, n_cols = spec.shape[1:]
    at = pair_rows(n_rows, pair)
    near = frame.shape[2] - EDGE

    def store(cols, w, c, value):
        frame[w, c, :EDGE, cols] = value

    spectral_rows(keep, halo, corners, store, chan_count, n_cols, slice(None))
    inner = pl.multiple_of(jnp.where(at == 0, 0, n_rows - near), EDGE)
    frame[:, :, EDGE:, :] = spec[:, :, pl.ds(inner, near), :]
    which = jnp.where(at == 0, 0, 1)

    def add(w, f, c, total):
        acc[smooth_slot(chan_count, w, f, c) - 2 * chan_count] = total

    row_pass(lambda: row_band[which], lambda w, c: frame[w, c], rowwise, chan_count, 4)
    column_pass(rowwise, matrix, smooth, add, chan_count)
    before = sums[: 2 * chan_count, :]
    total = sums[2 * chan_count :, :] + jnp.sum(acc[...], axis=1)
    if pair == 0:
        sums_out[: 2 * chan_count, :] = before
        sums_out[2 * chan_count :, :] = total
    else:
        sums_out[...] = share(jnp.concatenate([before, total]), sums_out)


def share(acc_sum, out):
    peers, width = out.shape
    slots = acc_sum.shape[0]
    if slots < width:
        acc_sum = jnp.concatenate([acc_sum, jnp.zeros((width - slots, LANES), f32)], axis=0)
    total = jnp.sum(acc_sum.T, axis=0, keepdims=True)
    return jnp.broadcast_to(total, (peers, width))


def spread(shared):
    total = jnp.sum(shared[...], axis=0, keepdims=True)
    return jnp.broadcast_to(total, (LANES, total.shape[1])).T


def clip_kernel(pixels, shared_in, spec, middle, edge_one, edge_two, shared, limit, acc):
    chan_count = spec.shape[1]
    rough = jnp.sqrt(spread(shared_in) / pixels + epsilon)
    limit[...] = (clip_level * rough) ** 2

    @pl.loop(0, chan_count)
    def _(c):
        def clipped(slot, parts):
            top = wide(limit, slot, 8)
            total = None
            for part in parts:
                for r in range(0, part.shape[0], 8):
                    for l in range(0, part.shape[1], LANES):
                        value = part[r : r + 8, l : l + LANES]
                        value = jnp.minimum(value * value, top)
                        total = value if total is None else total + value
            acc[slot] = total

        for w in range(2):
            clipped(spectral_slot(chan_count, w, c), [spec[w, c].astype(f32)])
            for f in range(2):
                parts = []
                for source in (middle, edge_one, edge_two):
                    per = source.shape[1] // (2 * chan_count)
                    start = pl.multiple_of((w * chan_count + c) * per, per)
                    parts.append(source[f, pl.ds(start, per), :])
                clipped(smooth_slot(chan_count, w, f, c), parts)

    shared[...] = share(jnp.sum(acc[...], axis=1), shared)


def ratio_kernel(pixels, keep, shared_in, spec, middle, edge_one, edge_two, out, scale, staged, sems):
    chan_count, n_rows, n_cols = out.shape
    scale[...] = 1.0 / jnp.sqrt(spread(shared_in) / pixels + epsilon)
    parts = sems.shape[0]
    group = chan_count // parts
    tiles = [(middle, r, EDGE + r) for r in range(0, n_rows - 2 * EDGE, EDGE)]
    tiles += [(edge_one, 0, pair_rows(n_rows, 0)), (edge_two, 0, pair_rows(n_rows, 1))]

    def channel(c):
        keep_tile = wide(keep, c)
        factors = [
            [wide(scale, spectral_slot(chan_count, w, c))]
            + [wide(scale, smooth_slot(chan_count, w, f, c)) for f in range(2)]
            for w in range(2)
        ]
        for source, offset, row in tiles:
            rows = pl.ds(row, EDGE)
            per = source.shape[1] // (2 * chan_count)
            for l in range(0, n_cols, LANES):
                cols = slice(l, l + LANES)
                best = None
                for w in range(2):
                    start = pl.multiple_of((w * chan_count + c) * per + offset, EDGE)
                    values = [spec[w, c, rows, cols].astype(f32)]
                    values += [source[f, pl.ds(start, EDGE), cols] for f in range(2)]
                    for value, factor in zip(values, factors[w]):
                        value = value * factor
                        best = value if best is None else jnp.maximum(best, value)
                staged[c, rows, cols] = (best * keep_tile).astype(bf16)

    copies = []
    for p in range(parts):
        pl.loop(p * group, (p + 1) * group)(channel)
        s = slice(p * group, (p + 1) * group)
        copies.append(pltpu.make_async_copy(staged.at[s], out.at[s], sems.at[p]))
        copies[-1].start()
    for copy in copies:
        copy.wait()


def specs(spaces):
    return [pl.BlockSpec(memory_space=s) for s in spaces]


def call(kernel, ins, outs, scratch, flops, out_space=VMEM):
    return pl.pallas_call(
        kernel,
        in_specs=specs(ins),
        out_specs=specs([out_space] * len(outs)),
        out_shape=[jax.ShapeDtypeStruct(s, d) for s, d in outs],
        scratch_shapes=scratch,
        compiler_params=pltpu.CompilerParams(vmem_limit_bytes=32 * 2**20),
        cost_estimate=pl.CostEstimate(flops=flops, bytes_accessed=2**20, transcendentals=0),
    )


def shards(sky_cube, chan_flags):
    chan_count, n_rows, n_cols = sky_cube.shape
    strips, blocks = lax.axis_size("strip"), lax.axis_size("chan")
    pixels = n_rows * strips * n_cols
    turns = 1 if blocks == 2 else 2
    slots = 6 * chan_count
    width = -(-slots // LANES) * LANES
    mid = n_rows - 2 * EDGE
    near = 2 * EDGE
    dma = pltpu.SemaphoreType.DMA

    own_rows = np.arange(n_rows)
    mid_band = constant(band(own_rows[EDGE : n_rows - EDGE], own_rows).reshape(2 * mid, n_rows))
    top = band(np.arange(EDGE), np.concatenate([np.arange(-EDGE, 0), np.arange(near)]))
    bottom = band(np.arange(near - EDGE, near), np.concatenate([np.arange(near, near + EDGE), np.arange(near)]))
    edge_band = constant(np.stack([top, bottom]).reshape(2, 2 * EDGE, EDGE + near))
    cols = np.arange(n_cols)
    taps = band(cols, cols).transpose(0, 2, 1)
    same = cols[:, None] // BLOCK == cols[None, :] // BLOCK
    starts = np.arange(0, n_cols, BLOCK)
    pieces = [(taps * same)[:, b : b + BLOCK, b : b + BLOCK] for b in starts]
    pieces += [(taps * ~same)[:, b : b + BLOCK, b : b + BLOCK] for b in starts[:-1] + LANES]
    matrix = constant(np.stack(pieces, axis=1))

    sky_cube, chan_flags, mid_band, edge_band, matrix = (
        pltpu.with_memory_space_constraint(v, HBM)
        for v in (sky_cube, chan_flags, mid_band, edge_band, matrix)
    )

    edge_rows = ((chan_count, EDGE, n_cols), bf16)
    first_pair, second_pair = call(
        pick_kernel, [HBM], [edge_rows, edge_rows], [dma((2,))], 10**6
    )(sky_cube)

    evens = [(i, i + 1) for i in range(0, strips - 1, 2)]
    odds = [(i, i + 1) for i in range(1, strips - 1, 2)]
    evens, odds = (p + [(b, a) for a, b in p] for p in (evens, odds))
    first_pair = lax.ppermute(first_pair, "strip", evens)
    second_pair = lax.ppermute(second_pair, "strip", odds)

    forth = [(i, i + 1) for i in range(blocks - 1)]
    back = [(j, i) for i, j in forth]
    moves = [forth + back] if turns == 1 else [forth, back]

    def across(payload):
        sent = [lax.ppermute(payload[i : i + 1], "chan", p) for i, p in enumerate(moves)]
        return jnp.concatenate(sent)

    rims, keep = call(
        rim_kernel,
        [HBM, HBM],
        [((turns, RIM, n_rows, n_cols), bf16), ((chan_count + 8, LANES), f32)],
        [
            SMEM((chan_count,), jnp.int32),
            VMEM((turns, RIM, n_rows, n_cols), bf16),
            dma((turns + 1,)),
        ],
        10**6,
    )(chan_flags, sky_cube)
    rim = across(rims)
    own, mid_band, edge_band, matrix = call(
        load_kernel,
        [HBM] * 4,
        [(v.shape, bf16) for v in (sky_cube, mid_band, edge_band, matrix)],
        [dma((4,))],
        10**6,
    )(sky_cube, mid_band, edge_band, matrix)

    def corners_of(halo):
        (corners,) = call(
            corner_kernel, [VMEM] * 2, [((turns, RIM, EDGE, n_cols), bf16)], [], 10**6
        )(keep, halo)
        return across(corners)

    corners_one = corners_of(first_pair)
    corners_two = corners_of(second_pair)
    spec, middle, sums = call(
        middle_kernel,
        [VMEM] * 5,
        [
            ((2, chan_count, n_rows, n_cols), bf16),
            ((2, 2 * chan_count * mid, n_cols), f32),
            ((slots, LANES), f32),
        ],
        [VMEM((2, 2 * chan_count * mid, n_cols), bf16), VMEM((slots, 8, LANES), f32)],
        2 * 10**9,
    )(keep, own, rim, mid_band, matrix)

    edge_out = ((2, 2 * chan_count * EDGE, n_cols), f32)
    edge_scratch = [
        VMEM((2, 2 * chan_count * EDGE, n_cols), bf16),
        VMEM((slots - 2 * chan_count, 8, LANES), f32),
        VMEM((2, chan_count, EDGE + near, n_cols), bf16),
    ]
    edge_one, sums = call(
        functools.partial(edge_kernel, 0),
        [VMEM] * 7,
        [edge_out, ((slots, LANES), f32)],
        edge_scratch,
        10**9,
    )(keep, first_pair, corners_one, spec, edge_band, matrix, sums)
    edge_two, shared = call(
        functools.partial(edge_kernel, 1),
        [VMEM] * 7,
        [edge_out, ((strips, width), f32)],
        edge_scratch,
        10**9,
    )(keep, second_pair, corners_two, spec, edge_band, matrix, sums)

    shared = lax.all_to_all(shared, "strip", 0, 0, tiled=True)
    (shared,) = call(
        functools.partial(clip_kernel, pixels),
        [VMEM] * 5,
        [((strips, width), f32)],
        [VMEM((width, LANES), f32), VMEM((slots, 8, LANES), f32)],
        10**8,
    )(shared, spec, middle, edge_one, edge_two)
    shared = lax.all_to_all(shared, "strip", 0, 0, tiled=True)
    (out,) = call(
        functools.partial(ratio_kernel, pixels),
        [VMEM] * 6,
        [((chan_count, n_rows, n_cols), bf16)],
        [VMEM((width, LANES), f32), VMEM((chan_count, n_rows, n_cols), bf16), dma((4,))],
        10**8,
        HBM,
    )(keep, shared, spec, middle, edge_one, edge_two)
    return out


def solution(mesh):
    in_specs = (P("chan", "strip", "groups"), P("chan"))
    out_specs = P("chan", "strip", "groups")
    return jax.shard_map(shards, mesh=mesh, in_specs=in_specs, out_specs=out_specs, check_vma=False)
```

```python
import functools
import math

import jax
import jax.numpy as jnp
import numpy as np
from jax import lax
from jax.experimental import pallas as pl
from jax.experimental.pallas import tpu as pltpu
from jax.sharding import PartitionSpec as P

gauss_settings = ((5.0, 8), (10.0, 15))
epsilon = 1e-06
clip_level = 3.0
RIM = 3
REACH = 15
EDGE = 16
LANES = 128
BLOCK = 2 * LANES
VMEM, HBM, SMEM = pltpu.VMEM, pltpu.HBM, pltpu.SMEM
f32, bf16 = jnp.float32, jnp.bfloat16


def gauss_weights(fwhm, radius):
    offsets = np.arange(-REACH, REACH + 1)
    spread = fwhm / (2.0 * math.sqrt(2.0 * math.log(2.0)))
    weights = np.exp(-(offsets**2) / (2.0 * spread**2)) * (np.abs(offsets) <= radius)
    weights = weights / weights.sum()
    return weights.astype(np.float32)


def band(out_positions, in_positions):
    offset = np.asarray(in_positions)[None, :] - np.asarray(out_positions)[:, None]
    inside = np.abs(offset) <= REACH
    index = np.clip(offset + REACH, 0, 2 * REACH)
    return np.stack([np.where(inside, gauss_weights(*s)[index], 0.0) for s in gauss_settings])


def constant(matrix):
    return jnp.asarray(matrix.astype(np.float32)).astype(bf16)


def fold(values):
    rows, cols = values.shape
    total = None
    for r in range(0, rows, 8):
        for c in range(0, cols, LANES):
            part = values[r : r + 8, c : c + LANES]
            total = part if total is None else total + part
    return total


def wide(ref, row, rows=EDGE):
    return jnp.broadcast_to(ref[pl.ds(row, 1), :], (rows, LANES))


def towards(chan_count, turns):
    last = chan_count - RIM
    if turns == 1:
        return [jnp.where(lax.axis_index("chan") == 0, last, 0)]
    return [last, 0]


def rest(chan_count, turns):
    if turns == 1:
        return jnp.where(lax.axis_index("chan") == 0, 0, RIM), chan_count - RIM
    return RIM, chan_count - 2 * RIM


def pair_rows(n_rows, pair):
    odd = lax.rem(lax.axis_index("strip"), 2)
    at_end = odd == pair
    return pl.multiple_of(jnp.where(at_end, n_rows - EDGE, 0), EDGE)


def spectral_slot(chan_count, w, c):
    return w * chan_count + c


def smooth_slot(chan_count, w, f, c):
    return (2 + 2 * w + f) * chan_count + c


def means(x):
    for i in range(RIM, len(x) - RIM):
        s3 = x[i - 1] + x[i] + x[i + 1]
        s7 = (x[i - 3] + x[i - 2]) + s3 + (x[i + 2] + x[i + 3])
        yield i - RIM, [(s3 * (1.0 / 3.0)).astype(bf16), (s7 * (1.0 / 7.0)).astype(bf16)]


def row_pass(taps, plane, rowwise, slots, count, at=0):
    per = taps.shape[0] // 2
    for i in range(count):
        row = jnp.dot(taps, plane(slots[i]), preferred_element_type=f32).astype(bf16)
        start = (at + i) * per
        if not isinstance(start, int):
            start = pl.multiple_of(start, per)
        for f in range(2):
            rowwise[f, pl.ds(start, per), :] = row[f * per : (f + 1) * per]


def column_pass(rowwise, matrix, count, put):
    n_cols = rowwise.shape[2]
    per = rowwise.shape[1] // count
    blocks = n_cols // BLOCK
    for f in range(2):
        products = []
        for i in range(2 * blocks - 1):
            b = i * BLOCK if i < blocks else (i - blocks) * BLOCK + LANES
            x = rowwise[f, :, b : b + BLOCK]
            products.append(jnp.dot(x, matrix[f, i], preferred_element_type=f32))
        diagonal, seams = products[:blocks], products[blocks:]
        for slot in range(count):
            rows = slice(slot * per, (slot + 1) * per)
            values = []
            for l in range(0, n_cols, LANES):
                b, right = l // BLOCK, l % BLOCK
                value = diagonal[b][rows, right : right + LANES]
                if right and b < len(seams):
                    value = value + seams[b][rows, :LANES]
                if not right and b > 0:
                    value = value + seams[b - 1][rows, LANES:]
                values.append(value)
            put(f, slot, values)


def put_tiles(smooth, squares, acc, f, start, slot, values):
    rows = pl.ds(start, values[0].shape[0])
    total = None
    for i, value in enumerate(values):
        cols = slice(i * LANES, (i + 1) * LANES)
        square = value * value
        smooth[f, rows, cols] = value
        squares[f, rows, cols] = square
        part = fold(square)
        total = part if total is None else total + part
    acc[slot] = total


def run(copies):
    for copy in copies:
        copy.start()
    for copy in copies:
        copy.wait()


def pick_kernel(sky, first_pair, second_pair, sems):
    pieces = (first_pair, second_pair)
    rows = [pl.ds(pair_rows(sky.shape[1], pair), EDGE) for pair in range(2)]
    run(
        [
            pltpu.make_async_copy(sky.at[:, rows[pair], :], pieces[pair], sems.at[pair])
            for pair in range(2)
        ]
    )


def rim_kernel(flags, sky, rims, keep, flag, raw, sems):
    chan_count, _, _ = sky.shape
    turns = rims.shape[0]
    first = towards(chan_count, turns)
    copies = [pltpu.make_async_copy(flags, flag, sems.at[turns])]
    for turn in range(turns):
        source = sky.at[pl.ds(first[turn], RIM)]
        copies.append(pltpu.make_async_copy(source, raw.at[turn], sems.at[turn]))
    run(copies)
    block = lax.axis_index("chan")
    before = (block > 0).astype(jnp.int32)
    after = (block < lax.axis_size("chan") - 1).astype(jnp.int32)
    factors = [before] * RIM + [1 - flag[c] for c in range(chan_count)] + [after] * RIM
    for i, factor in enumerate(factors):
        keep[i : i + 1, :] = jnp.full((1, LANES), factor.astype(f32), f32)
    for turn in range(turns):
        for i in range(RIM):
            factor = (1 - flag[first[turn] + i]).astype(f32)
            rims[turn, i] = (raw[turn, i].astype(f32) * factor).astype(bf16)


def load_kernel(sky, mid_in, edge_in, matrix_in, own, mid_band, edge_band, matrix, sems):
    run(
        [
            pltpu.make_async_copy(sky, own, sems.at[0]),
            pltpu.make_async_copy(matrix_in, matrix, sems.at[1]),
            pltpu.make_async_copy(mid_in, mid_band, sems.at[2]),
            pltpu.make_async_copy(edge_in, edge_band, sems.at[3]),
        ]
    )


def corner_kernel(keep, halo, corners):
    chan_count, _, n_cols = halo.shape
    for turn, first in enumerate(towards(chan_count, corners.shape[0])):
        for i in range(RIM):
            factor = wide(keep, RIM + first + i)
            for l in range(0, n_cols, LANES):
                cols = slice(l, l + LANES)
                corners[turn, i, :, cols] = (halo[first + i, :, cols].astype(f32) * factor).astype(bf16)


def middle_kernel(keep, sky, rim, row_band, matrix, spec, spec_squares, smooth, squares, sums, rowwise, acc):
    chan_count, n_rows, n_cols = sky.shape
    per = n_rows - 2 * EDGE

    @pl.loop(0, n_rows // EDGE)
    def _(t):
        rows = pl.ds(pl.multiple_of(t * EDGE, EDGE), EDGE)
        for lane in range(0, n_cols, LANES):
            cols = slice(lane, lane + LANES)
            x = [rim[0, i, rows, cols] for i in range(RIM)]
            x += [sky[c, rows, cols] for c in range(chan_count)]
            x += [rim[rim.shape[0] - 1, i, rows, cols] for i in range(RIM)]
            x = [value.astype(f32) * wide(keep, i) for i, value in enumerate(x)]
            for c, both in means(x):
                for w in range(2):
                    spec[w, c, rows, cols] = both[w]

    group = 4

    @pl.loop(0, chan_count // group)
    def _(g):
        for w in range(2):

            def plane(c):
                value = spec[w, c]
                exact = value.astype(f32)
                square = exact * exact
                spec_squares[w, c] = square
                acc[spectral_slot(chan_count, w, c)] = fold(square)
                return value

            c = [g * group + i for i in range(group)]
            row_pass(row_band[...], plane, rowwise, c, group, w * chan_count + g * group)

    def put(f, slot, values):
        w, c = slot // chan_count, slot % chan_count
        target = smooth_slot(chan_count, w, f, c)
        put_tiles(smooth, squares, acc, f, slot * per, target, values)

    column_pass(rowwise, matrix, 2 * chan_count, put)
    sums[...] = jnp.sum(acc[...], axis=1)


def edge_kernel(pair, turns, inner, rims, peers, *refs):
    refs = list(refs)
    keep, halo = refs[:2]
    del refs[:2]
    corners = refs.pop(0) if rims else None
    spec, row_band, matrix, sums = refs[:4]
    if rims and not inner:
        del refs[4:6]
    smooth, squares, sums_out, rowwise, acc, frame = refs[-6:]
    chan_count, n_rows, n_cols = spec.shape[1:]
    near = frame.shape[2] - EDGE
    at = pair_rows(n_rows, pair)
    inside = pl.multiple_of(jnp.where(at == 0, 0, n_rows - near), EDGE)
    groups = []
    if inner:
        groups.append(rest(chan_count, turns) + (None,))
    if rims:
        for turn, first in enumerate(towards(chan_count, turns)):
            groups.append((first, RIM, turn))

    channels = []
    for first, count, turn in groups:
        base = len(channels)
        channels += [first + i for i in range(count)]
        for lane in range(0, n_cols, LANES):
            cols = slice(lane, lane + LANES)
            x = []
            for i in range(count + 2 * RIM):
                c = first - RIM + i
                value = halo[jnp.clip(c, 0, chan_count - 1), :, cols].astype(f32)
                if turn is not None and (i < RIM or i >= count + RIM):
                    other = corners[turns - 1 - turn, i if i < RIM else i - count - RIM, :, cols]
                    own = jnp.logical_and(c >= 0, c < chan_count)
                    value = jnp.where(own, value, other.astype(f32))
                x.append(value * wide(keep, RIM + c))
            for i, both in means(x):
                for w in range(2):
                    frame[w, base + i, :EDGE, cols] = both[w]
        for w in range(2):
            frame[w, base : base + count, EDGE:, :] = spec[w, pl.ds(first, count), pl.ds(inside, near), :]

    count = len(channels)
    taps = row_band[jnp.where(at == 0, 0, 1)]
    for w in range(2):
        row_pass(taps, lambda i: frame[w, i], rowwise, list(range(count)), count, w * count)
    if count < chan_count:
        acc[...] = jnp.zeros_like(acc)

    def put(f, slot, values):
        w, c = slot // count, channels[slot % count]
        start = pl.multiple_of((w * chan_count + c) * EDGE, EDGE)
        target = smooth_slot(chan_count, w, f, c) - 2 * chan_count
        put_tiles(smooth, squares, acc, f, start, target, values)

    column_pass(rowwise, matrix, 2 * count, put)
    before = sums[: 2 * chan_count, :]
    total = sums[2 * chan_count :, :] + jnp.sum(acc[...], axis=1)
    if peers:
        sums_out[...] = share(jnp.concatenate([before, total]), sums_out)
    else:
        sums_out[: 2 * chan_count, :] = before
        sums_out[2 * chan_count :, :] = total


def share(acc_sum, out):
    peers, width = out.shape
    slots = acc_sum.shape[0]
    if slots < width:
        acc_sum = jnp.concatenate([acc_sum, jnp.zeros((width - slots, LANES), f32)], axis=0)
    total = jnp.sum(acc_sum.T, axis=0, keepdims=True)
    return jnp.broadcast_to(total, (peers, width))


def spread(shared):
    total = jnp.sum(shared[...], axis=0, keepdims=True)
    return jnp.broadcast_to(total, (LANES, total.shape[1])).T


def clip_kernel(pixels, shared_in, spec, middle, edge_one, edge_two, shared, limit, acc):
    chan_count = spec.shape[1]
    rough = jnp.sqrt(spread(shared_in) / pixels + epsilon)
    limit[...] = (clip_level * rough) ** 2

    @pl.loop(0, chan_count)
    def _(c):
        def clipped(slot, parts):
            top = wide(limit, slot, 8)
            total = None
            for part in parts:
                for r in range(0, part.shape[0], 8):
                    for l in range(0, part.shape[1], LANES):
                        value = jnp.minimum(part[r : r + 8, l : l + LANES], top)
                        total = value if total is None else total + value
            acc[slot] = total

        for w in range(2):
            clipped(spectral_slot(chan_count, w, c), [spec[w, c]])
            for f in range(2):
                parts = []
                for source in (middle, edge_one, edge_two):
                    per = source.shape[1] // (2 * chan_count)
                    start = pl.multiple_of((w * chan_count + c) * per, per)
                    parts.append(source[f, pl.ds(start, per), :])
                clipped(smooth_slot(chan_count, w, f, c), parts)

    shared[...] = share(jnp.sum(acc[...], axis=1), shared)


def ratio_kernel(pixels, keep, shared_in, spec, middle, edge_one, edge_two, out, scale, staged, sems):
    chan_count, n_rows, n_cols = out.shape
    scale[...] = 1.0 / jnp.sqrt(spread(shared_in) / pixels + epsilon)
    for k in range(6):
        rows = slice(k * chan_count, (k + 1) * chan_count)
        scale[rows, :] = scale[rows, :] * keep[RIM : RIM + chan_count, :]
    parts = sems.shape[0]
    group = chan_count // parts
    tiles = [(middle, r, EDGE + r) for r in range(0, n_rows - 2 * EDGE, EDGE)]
    tiles += [(edge_one, 0, pair_rows(n_rows, 0)), (edge_two, 0, pair_rows(n_rows, 1))]

    def channel(c):
        factors = [
            [wide(scale, spectral_slot(chan_count, w, c))]
            + [wide(scale, smooth_slot(chan_count, w, f, c)) for f in range(2)]
            for w in range(2)
        ]
        for source, offset, row in tiles:
            rows = pl.ds(row, EDGE)
            per = source.shape[1] // (2 * chan_count)
            for l in range(0, n_cols, LANES):
                cols = slice(l, l + LANES)
                best = None
                for w in range(2):
                    start = pl.multiple_of((w * chan_count + c) * per + offset, EDGE)
                    values = [spec[w, c, rows, cols].astype(f32)]
                    values += [source[f, pl.ds(start, EDGE), cols] for f in range(2)]
                    for value, factor in zip(values, factors[w]):
                        value = value * factor
                        best = value if best is None else jnp.maximum(best, value)
                staged[c, rows, cols] = best.astype(bf16)

    copies = []
    for p in range(parts):
        pl.loop(p * group, (p + 1) * group)(channel)
        s = slice(p * group, (p + 1) * group)
        copies.append(pltpu.make_async_copy(staged.at[s], out.at[s], sems.at[p]))
        copies[-1].start()
    for copy in copies:
        copy.wait()


def specs(spaces):
    return [pl.BlockSpec(memory_space=s) for s in spaces]


def call(kernel, ins, outs, scratch, flops, out_space=VMEM, aliases={}):
    return pl.pallas_call(
        kernel,
        in_specs=specs(ins),
        out_specs=specs([out_space] * len(outs)),
        out_shape=[jax.ShapeDtypeStruct(s, d) for s, d in outs],
        scratch_shapes=scratch,
        input_output_aliases=aliases,
        compiler_params=pltpu.CompilerParams(vmem_limit_bytes=32 * 2**20),
        cost_estimate=pl.CostEstimate(flops=flops, bytes_accessed=2**20, transcendentals=0),
    )


def shards(sky_cube, chan_flags):
    chan_count, n_rows, n_cols = sky_cube.shape
    strips, blocks = lax.axis_size("strip"), lax.axis_size("chan")
    pixels = n_rows * strips * n_cols
    turns = 1 if blocks == 2 else 2
    slots = 6 * chan_count
    width = -(-slots // LANES) * LANES
    mid = n_rows - 2 * EDGE
    near = 2 * EDGE
    dma = pltpu.SemaphoreType.DMA

    own_rows = np.arange(n_rows)
    mid_band = constant(band(own_rows[EDGE : n_rows - EDGE], own_rows).reshape(2 * mid, n_rows))
    top = band(np.arange(EDGE), np.concatenate([np.arange(-EDGE, 0), np.arange(near)]))
    bottom = band(np.arange(near - EDGE, near), np.concatenate([np.arange(near, near + EDGE), np.arange(near)]))
    edge_band = constant(np.stack([top, bottom]).reshape(2, 2 * EDGE, EDGE + near))
    cols = np.arange(n_cols)
    taps = band(cols, cols).transpose(0, 2, 1)
    same = cols[:, None] // BLOCK == cols[None, :] // BLOCK
    starts = np.arange(0, n_cols, BLOCK)
    pieces = [(taps * same)[:, b : b + BLOCK, b : b + BLOCK] for b in starts]
    pieces += [(taps * ~same)[:, b : b + BLOCK, b : b + BLOCK] for b in starts[:-1] + LANES]
    matrix = constant(np.stack(pieces, axis=1))

    sky_cube, chan_flags, mid_band, edge_band, matrix = (
        pltpu.with_memory_space_constraint(v, HBM)
        for v in (sky_cube, chan_flags, mid_band, edge_band, matrix)
    )

    edge_rows = ((chan_count, EDGE, n_cols), bf16)
    first_pair, second_pair = call(
        pick_kernel, [HBM], [edge_rows, edge_rows], [dma((2,))], 10**6
    )(sky_cube)

    evens = [(i, i + 1) for i in range(0, strips - 1, 2)]
    odds = [(i, i + 1) for i in range(1, strips - 1, 2)]
    evens, odds = (p + [(b, a) for a, b in p] for p in (evens, odds))
    first_pair = lax.ppermute(first_pair, "strip", evens)
    second_pair = lax.ppermute(second_pair, "strip", odds)

    forth = [(i, i + 1) for i in range(blocks - 1)]
    back = [(j, i) for i, j in forth]
    moves = [forth + back] if turns == 1 else [forth, back]

    def across(payload):
        sent = [lax.ppermute(payload[i : i + 1], "chan", p) for i, p in enumerate(moves)]
        return jnp.concatenate(sent)

    rims, keep = call(
        rim_kernel,
        [HBM, HBM],
        [((turns, RIM, n_rows, n_cols), bf16), ((chan_count + 2 * RIM, LANES), f32)],
        [
            SMEM((chan_count,), jnp.int32),
            VMEM((turns, RIM, n_rows, n_cols), bf16),
            dma((turns + 1,)),
        ],
        10**6,
    )(chan_flags, sky_cube)
    rim = across(rims)
    own, mid_band, edge_band, matrix = call(
        load_kernel,
        [HBM] * 4,
        [(v.shape, bf16) for v in (sky_cube, mid_band, edge_band, matrix)],
        [dma((4,))],
        10**6,
    )(sky_cube, mid_band, edge_band, matrix)

    def corners_of(halo):
        (corners,) = call(
            corner_kernel, [VMEM] * 2, [((turns, RIM, EDGE, n_cols), bf16)], [], 10**6
        )(keep, halo)
        return across(corners)

    corners_one = corners_of(first_pair)

    mid_out = ((2, 2 * chan_count * mid, n_cols), f32)
    sums_out = ((slots, LANES), f32)
    spec, spec_squares, middle, middle_squares, sums = call(
        middle_kernel,
        [VMEM] * 5,
        [
            ((2, chan_count, n_rows, n_cols), bf16),
            ((2, chan_count, n_rows, n_cols), f32),
            mid_out,
            mid_out,
            sums_out,
        ],
        [VMEM(mid_out[0], bf16), VMEM((slots, 8, LANES), f32)],
        2 * 10**9,
    )(keep, own, rim, mid_band, matrix)

    def edge(pair, inner, rims, last, *args):
        count = (chan_count - turns * RIM) * inner + turns * RIM * rims
        in_place = rims and not inner
        out = ((2, 2 * chan_count * EDGE, n_cols), f32)
        return call(
            functools.partial(edge_kernel, pair, turns, inner, rims, last),
            [VMEM] * len(args),
            [out, out, ((strips, width), f32) if last else sums_out],
            [
                VMEM((2, 2 * count * EDGE, n_cols), bf16),
                VMEM((slots - 2 * chan_count, 8, LANES), f32),
                VMEM((2, count, EDGE + near, n_cols), bf16),
            ],
            10**9,
            aliases={len(args) - 2: 0, len(args) - 1: 1} if in_place else {},
        )(*args)

    edge_one, one_squares, sums = edge(
        0, True, True, False, keep, first_pair, corners_one, spec, edge_band, matrix, sums
    )
    corners_two = corners_of(second_pair)
    edge_two, two_squares, sums = edge(
        1, True, False, False, keep, second_pair, spec, edge_band, matrix, sums
    )
    edge_two, two_squares, shared = edge(
        1, False, True, True, keep, second_pair, corners_two, spec, edge_band, matrix, sums,
        edge_two, two_squares,
    )

    shared = lax.all_to_all(shared, "strip", 0, 0, tiled=True)
    (shared,) = call(
        functools.partial(clip_kernel, pixels),
        [VMEM] * 5,
        [((strips, width), f32)],
        [VMEM((width, LANES), f32), VMEM((slots, 8, LANES), f32)],
        10**8,
    )(shared, spec_squares, middle_squares, one_squares, two_squares)
    shared = lax.all_to_all(shared, "strip", 0, 0, tiled=True)
    (out,) = call(
        functools.partial(ratio_kernel, pixels),
        [VMEM] * 6,
        [((chan_count, n_rows, n_cols), bf16)],
        [VMEM((width, LANES), f32), VMEM((chan_count, n_rows, n_cols), bf16), dma((4,))],
        10**8,
        HBM,
    )(keep, shared, spec, middle, edge_one, edge_two)
    return out


def solution(mesh):
    in_specs = (P("chan", "strip", "groups"), P("chan"))
    out_specs = P("chan", "strip", "groups")
    return jax.shard_map(shards, mesh=mesh, in_specs=in_specs, out_specs=out_specs, check_vma=False)
```

```python
import functools
import math

import jax
import jax.numpy as jnp
import numpy as np
from jax import lax
from jax.experimental import pallas as pl
from jax.experimental.pallas import tpu as pltpu
from jax.sharding import PartitionSpec as P

gauss_settings = ((5.0, 8), (10.0, 15))
epsilon = 1e-06
clip_level = 3.0
RIM = 3
REACH = 15
EDGE = 16
LANES = 128
BLOCK = 2 * LANES
VMEM, HBM, SMEM = pltpu.VMEM, pltpu.HBM, pltpu.SMEM
f32, bf16 = jnp.float32, jnp.bfloat16


def gauss_weights(fwhm, radius):
    offsets = np.arange(-REACH, REACH + 1)
    spread = fwhm / (2.0 * math.sqrt(2.0 * math.log(2.0)))
    weights = np.exp(-(offsets**2) / (2.0 * spread**2)) * (np.abs(offsets) <= radius)
    weights = weights / weights.sum()
    return weights.astype(np.float32)


def band(out_positions, in_positions):
    offset = np.asarray(in_positions)[None, :] - np.asarray(out_positions)[:, None]
    inside = np.abs(offset) <= REACH
    index = np.clip(offset + REACH, 0, 2 * REACH)
    return np.stack([np.where(inside, gauss_weights(*s)[index], 0.0) for s in gauss_settings])


def constant(matrix):
    return jnp.asarray(matrix.astype(np.float32)).astype(bf16)


def fold(values):
    rows, cols = values.shape
    total = None
    for r in range(0, rows, 8):
        for c in range(0, cols, LANES):
            part = values[r : r + 8, c : c + LANES]
            total = part if total is None else total + part
    return total


def wide(ref, row, rows=EDGE):
    return jnp.broadcast_to(ref[pl.ds(row, 1), :], (rows, LANES))


def towards(chan_count, turns):
    last = chan_count - RIM
    if turns == 1:
        return [jnp.where(lax.axis_index("chan") == 0, last, 0)]
    return [last, 0]


def rest(chan_count, turns):
    if turns == 1:
        return jnp.where(lax.axis_index("chan") == 0, 0, RIM), chan_count - RIM
    return RIM, chan_count - 2 * RIM


def pair_rows(n_rows, pair):
    odd = lax.rem(lax.axis_index("strip"), 2)
    at_end = odd == pair
    return pl.multiple_of(jnp.where(at_end, n_rows - EDGE, 0), EDGE)


def spectral_slot(chan_count, w, c):
    return w * chan_count + c


def smooth_slot(chan_count, w, f, c):
    return (2 + 2 * w + f) * chan_count + c


def means(x):
    for i in range(RIM, len(x) - RIM):
        s3 = x[i - 1] + x[i] + x[i + 1]
        s7 = (x[i - 3] + x[i - 2]) + s3 + (x[i + 2] + x[i + 3])
        yield i - RIM, [(s3 * (1.0 / 3.0)).astype(bf16), (s7 * (1.0 / 7.0)).astype(bf16)]


def row_pass(taps, plane, rowwise, slots, count, at=0):
    per = taps.shape[0] // 2
    for i in range(count):
        row = jnp.dot(taps, plane(slots[i]), preferred_element_type=f32).astype(bf16)
        start = (at + i) * per
        if not isinstance(start, int):
            start = pl.multiple_of(start, per)
        for f in range(2):
            rowwise[f, pl.ds(start, per), :] = row[f * per : (f + 1) * per]


def column_pass(rowwise, matrix, count, put):
    n_cols = rowwise.shape[2]
    per = rowwise.shape[1] // count
    blocks = n_cols // BLOCK
    for f in range(2):
        products = []
        for i in range(2 * blocks - 1):
            b = i * BLOCK if i < blocks else (i - blocks) * BLOCK + LANES
            x = rowwise[f, :, b : b + BLOCK]
            products.append(jnp.dot(x, matrix[f, i], preferred_element_type=f32))
        diagonal, seams = products[:blocks], products[blocks:]
        for slot in range(count):
            rows = slice(slot * per, (slot + 1) * per)
            values = []
            for l in range(0, n_cols, LANES):
                b, right = l // BLOCK, l % BLOCK
                value = diagonal[b][rows, right : right + LANES]
                if right and b < len(seams):
                    value = value + seams[b][rows, :LANES]
                if not right and b > 0:
                    value = value + seams[b - 1][rows, LANES:]
                values.append(value)
            put(f, slot, values)


def put_tiles(smooth, squares, acc, f, start, slot, values, add=False):
    rows = pl.ds(start, values[0].shape[0])
    total = None
    for i, value in enumerate(values):
        cols = slice(i * LANES, (i + 1) * LANES)
        square = value * value
        smooth[f, rows, cols] = value
        squares[f, rows, cols] = square
        part = fold(square)
        total = part if total is None else total + part
    acc[slot] = acc[slot] + total if add else total


def run(copies):
    for copy in copies:
        copy.start()
    for copy in copies:
        copy.wait()


def pick_kernel(sky, first_pair, second_pair, sems):
    pieces = (first_pair, second_pair)
    rows = [pl.ds(pair_rows(sky.shape[1], pair), EDGE) for pair in range(2)]
    run(
        [
            pltpu.make_async_copy(sky.at[:, rows[pair], :], pieces[pair], sems.at[pair])
            for pair in range(2)
        ]
    )


def rim_kernel(flags, sky, rims, keep, flag, raw, sems):
    chan_count, _, _ = sky.shape
    turns = rims.shape[0]
    first = towards(chan_count, turns)
    copies = [pltpu.make_async_copy(flags, flag, sems.at[turns])]
    for turn in range(turns):
        source = sky.at[pl.ds(first[turn], RIM)]
        copies.append(pltpu.make_async_copy(source, raw.at[turn], sems.at[turn]))
    run(copies)
    block = lax.axis_index("chan")
    before = (block > 0).astype(jnp.int32)
    after = (block < lax.axis_size("chan") - 1).astype(jnp.int32)
    factors = [before] * RIM + [1 - flag[c] for c in range(chan_count)] + [after] * RIM
    for i, factor in enumerate(factors):
        keep[i : i + 1, :] = jnp.full((1, LANES), factor.astype(f32), f32)
    for turn in range(turns):
        for i in range(RIM):
            factor = (1 - flag[first[turn] + i]).astype(f32)
            rims[turn, i] = (raw[turn, i].astype(f32) * factor).astype(bf16)


def load_kernel(sky, mid_in, edge_in, matrix_in, own, mid_band, edge_band, matrix, sems):
    run(
        [
            pltpu.make_async_copy(sky, own, sems.at[0]),
            pltpu.make_async_copy(matrix_in, matrix, sems.at[1]),
            pltpu.make_async_copy(mid_in, mid_band, sems.at[2]),
            pltpu.make_async_copy(edge_in, edge_band, sems.at[3]),
        ]
    )


def corner_kernel(keep, first_pair, second_pair, corners):
    chan_count, _, n_cols = first_pair.shape
    for turn, first in enumerate(towards(chan_count, corners.shape[0])):
        for pair, halo in enumerate((first_pair, second_pair)):
            for i in range(RIM):
                factor = wide(keep, RIM + first + i)
                for l in range(0, n_cols, LANES):
                    cols = slice(l, l + LANES)
                    value = halo[first + i, :, cols].astype(f32) * factor
                    corners[turn, pair * RIM + i, :, cols] = value.astype(bf16)


def middle_kernel(keep, sky, rim, row_band, matrix, spec, spec_squares, smooth, squares, sums, rowwise, acc):
    chan_count, n_rows, n_cols = sky.shape
    per = n_rows - 2 * EDGE

    @pl.loop(0, n_rows // EDGE)
    def _(t):
        rows = pl.ds(pl.multiple_of(t * EDGE, EDGE), EDGE)
        for lane in range(0, n_cols, LANES):
            cols = slice(lane, lane + LANES)
            x = [rim[0, i, rows, cols] for i in range(RIM)]
            x += [sky[c, rows, cols] for c in range(chan_count)]
            x += [rim[rim.shape[0] - 1, i, rows, cols] for i in range(RIM)]
            x = [value.astype(f32) * wide(keep, i) for i, value in enumerate(x)]
            for c, both in means(x):
                for w in range(2):
                    spec[w, c, rows, cols] = both[w]

    group = 4

    @pl.loop(0, chan_count // group)
    def _(g):
        for w in range(2):

            def plane(c):
                value = spec[w, c]
                exact = value.astype(f32)
                square = exact * exact
                spec_squares[w, c] = square
                acc[spectral_slot(chan_count, w, c)] = fold(square)
                return value

            c = [g * group + i for i in range(group)]
            row_pass(row_band[...], plane, rowwise, c, group, w * chan_count + g * group)

    def put(f, slot, values):
        w, c = slot // chan_count, slot % chan_count
        target = smooth_slot(chan_count, w, f, c)
        put_tiles(smooth, squares, acc, f, slot * per, target, values)

    column_pass(rowwise, matrix, 2 * chan_count, put)
    sums[...] = jnp.sum(acc[...], axis=1)


def edge_kernel(pairs, turns, rims, *refs):
    refs = list(refs)

    def take(count):
        taken = refs[:count]
        del refs[:count]
        return taken

    (keep,) = take(1)
    halos = take(len(pairs))
    corners = take(1)[0] if rims else None
    spec, row_band, matrix, sums = take(4)
    if rims:
        take(2 * len(pairs))
    outs = [take(2) for _ in pairs]
    sums_out, rowwise, acc, frame = refs
    chan_count, n_rows, n_cols = spec.shape[1:]
    near = frame.shape[2] - EDGE
    groups = [rest(chan_count, turns) + (None,)]
    if rims:
        groups = [(first, RIM, turn) for turn, first in enumerate(towards(chan_count, turns))]

    planes, taps = [], []
    for side, pair in enumerate(pairs):
        at = pair_rows(n_rows, pair)
        inside = pl.multiple_of(jnp.where(at == 0, 0, n_rows - near), EDGE)
        taps.append(row_band[jnp.where(at == 0, 0, 1)])
        halo = halos[side]
        for first, count, turn in groups:
            base = len(planes)
            planes += [(side, first + i) for i in range(count)]
            for lane in range(0, n_cols, LANES):
                cols = slice(lane, lane + LANES)
                x = []
                for i in range(count + 2 * RIM):
                    c = first - RIM + i
                    value = halo[jnp.clip(c, 0, chan_count - 1), :, cols].astype(f32)
                    if turn is not None and (i < RIM or i >= count + RIM):
                        at_rim = pair * RIM + (i if i < RIM else i - count - RIM)
                        other = corners[turns - 1 - turn, at_rim, :, cols]
                        own = jnp.logical_and(c >= 0, c < chan_count)
                        value = jnp.where(own, value, other.astype(f32))
                    x.append(value * wide(keep, RIM + c))
                for i, both in means(x):
                    for w in range(2):
                        frame[w, base + i, :EDGE, cols] = both[w]
            for w in range(2):
                inner = spec[w, pl.ds(first, count), pl.ds(inside, near), :]
                frame[w, base : base + count, EDGE:, :] = inner

    count = len(planes)
    each = count // len(pairs)
    for w in range(2):
        for side in range(len(pairs)):
            slots = list(range(side * each, (side + 1) * each))
            row_pass(taps[side], lambda i: frame[w, i], rowwise, slots, each, w * count + side * each)
    acc[...] = jnp.zeros_like(acc)

    def put(f, slot, values):
        w = slot // count
        side, c = planes[slot % count]
        start = pl.multiple_of((w * chan_count + c) * EDGE, EDGE)
        target = smooth_slot(chan_count, w, f, c) - 2 * chan_count
        put_tiles(*outs[side], acc, f, start, target, values, side > 0)

    column_pass(rowwise, matrix, 2 * count, put)
    before = sums[: 2 * chan_count, :]
    total = sums[2 * chan_count :, :] + jnp.sum(acc[...], axis=1)
    if rims:
        sums_out[...] = share(jnp.concatenate([before, total]), sums_out)
    else:
        sums_out[: 2 * chan_count, :] = before
        sums_out[2 * chan_count :, :] = total


def share(acc_sum, out):
    peers, width = out.shape
    slots = acc_sum.shape[0]
    if slots < width:
        acc_sum = jnp.concatenate([acc_sum, jnp.zeros((width - slots, LANES), f32)], axis=0)
    total = jnp.sum(acc_sum.T, axis=0, keepdims=True)
    return jnp.broadcast_to(total, (peers, width))


def spread(shared):
    total = jnp.sum(shared[...], axis=0, keepdims=True)
    return jnp.broadcast_to(total, (LANES, total.shape[1])).T


def clip_kernel(pixels, shared_in, spec, middle, edge_one, edge_two, shared, limit, acc):
    chan_count = spec.shape[1]
    rough = jnp.sqrt(spread(shared_in) / pixels + epsilon)
    limit[...] = (clip_level * rough) ** 2

    @pl.loop(0, chan_count)
    def _(c):
        def clipped(slot, parts):
            top = wide(limit, slot, 8)
            total = None
            for part in parts:
                for r in range(0, part.shape[0], 8):
                    for l in range(0, part.shape[1], LANES):
                        value = jnp.minimum(part[r : r + 8, l : l + LANES], top)
                        total = value if total is None else total + value
            acc[slot] = total

        for w in range(2):
            clipped(spectral_slot(chan_count, w, c), [spec[w, c]])
            for f in range(2):
                parts = []
                for source in (middle, edge_one, edge_two):
                    per = source.shape[1] // (2 * chan_count)
                    start = pl.multiple_of((w * chan_count + c) * per, per)
                    parts.append(source[f, pl.ds(start, per), :])
                clipped(smooth_slot(chan_count, w, f, c), parts)

    shared[...] = share(jnp.sum(acc[...], axis=1), shared)


def ratio_kernel(pixels, keep, shared_in, spec, middle, edge_one, edge_two, out, scale, staged, sems):
    chan_count, n_rows, n_cols = out.shape
    scale[...] = 1.0 / jnp.sqrt(spread(shared_in) / pixels + epsilon)
    for k in range(6):
        rows = slice(k * chan_count, (k + 1) * chan_count)
        scale[rows, :] = scale[rows, :] * keep[RIM : RIM + chan_count, :]
    parts = sems.shape[0]
    group = chan_count // parts
    tiles = [(middle, r, EDGE + r) for r in range(0, n_rows - 2 * EDGE, EDGE)]
    tiles += [(edge_one, 0, pair_rows(n_rows, 0)), (edge_two, 0, pair_rows(n_rows, 1))]

    def channel(c):
        factors = [
            [wide(scale, spectral_slot(chan_count, w, c))]
            + [wide(scale, smooth_slot(chan_count, w, f, c)) for f in range(2)]
            for w in range(2)
        ]
        for source, offset, row in tiles:
            rows = pl.ds(row, EDGE)
            per = source.shape[1] // (2 * chan_count)
            for l in range(0, n_cols, LANES):
                cols = slice(l, l + LANES)
                best = None
                for w in range(2):
                    start = pl.multiple_of((w * chan_count + c) * per + offset, EDGE)
                    values = [spec[w, c, rows, cols].astype(f32)]
                    values += [source[f, pl.ds(start, EDGE), cols] for f in range(2)]
                    for value, factor in zip(values, factors[w]):
                        value = value * factor
                        best = value if best is None else jnp.maximum(best, value)
                staged[c, rows, cols] = best.astype(bf16)

    copies = []
    for p in range(parts):
        pl.loop(p * group, (p + 1) * group)(channel)
        s = slice(p * group, (p + 1) * group)
        copies.append(pltpu.make_async_copy(staged.at[s], out.at[s], sems.at[p]))
        copies[-1].start()
    for copy in copies:
        copy.wait()


def specs(spaces):
    return [pl.BlockSpec(memory_space=s) for s in spaces]


def call(kernel, ins, outs, scratch, flops, out_space=VMEM, aliases={}):
    return pl.pallas_call(
        kernel,
        in_specs=specs(ins),
        out_specs=specs([out_space] * len(outs)),
        out_shape=[jax.ShapeDtypeStruct(s, d) for s, d in outs],
        scratch_shapes=scratch,
        input_output_aliases=aliases,
        compiler_params=pltpu.CompilerParams(vmem_limit_bytes=12 * 2**20),
        cost_estimate=pl.CostEstimate(flops=flops, bytes_accessed=2**20, transcendentals=0),
    )


def shards(sky_cube, chan_flags):
    chan_count, n_rows, n_cols = sky_cube.shape
    strips, blocks = lax.axis_size("strip"), lax.axis_size("chan")
    pixels = n_rows * strips * n_cols
    turns = 1 if blocks == 2 else 2
    slots = 6 * chan_count
    width = -(-slots // LANES) * LANES
    mid = n_rows - 2 * EDGE
    near = 2 * EDGE
    dma = pltpu.SemaphoreType.DMA

    own_rows = np.arange(n_rows)
    mid_band = constant(band(own_rows[EDGE : n_rows - EDGE], own_rows).reshape(2 * mid, n_rows))
    top = band(np.arange(EDGE), np.concatenate([np.arange(-EDGE, 0), np.arange(near)]))
    bottom = band(np.arange(near - EDGE, near), np.concatenate([np.arange(near, near + EDGE), np.arange(near)]))
    edge_band = constant(np.stack([top, bottom]).reshape(2, 2 * EDGE, EDGE + near))
    cols = np.arange(n_cols)
    taps = band(cols, cols).transpose(0, 2, 1)
    same = cols[:, None] // BLOCK == cols[None, :] // BLOCK
    starts = np.arange(0, n_cols, BLOCK)
    pieces = [(taps * same)[:, b : b + BLOCK, b : b + BLOCK] for b in starts]
    pieces += [(taps * ~same)[:, b : b + BLOCK, b : b + BLOCK] for b in starts[:-1] + LANES]
    matrix = constant(np.stack(pieces, axis=1))

    sky_cube, chan_flags, mid_band, edge_band, matrix = (
        pltpu.with_memory_space_constraint(v, HBM)
        for v in (sky_cube, chan_flags, mid_band, edge_band, matrix)
    )

    edge_rows = ((chan_count, EDGE, n_cols), bf16)
    first_pair, second_pair = call(
        pick_kernel, [HBM], [edge_rows, edge_rows], [dma((2,))], 10**6
    )(sky_cube)

    evens = [(i, i + 1) for i in range(0, strips - 1, 2)]
    odds = [(i, i + 1) for i in range(1, strips - 1, 2)]
    evens, odds = (p + [(b, a) for a, b in p] for p in (evens, odds))
    first_pair = lax.ppermute(first_pair, "strip", evens)
    second_pair = lax.ppermute(second_pair, "strip", odds)

    forth = [(i, i + 1) for i in range(blocks - 1)]
    back = [(j, i) for i, j in forth]
    moves = [forth + back] if turns == 1 else [forth, back]

    def across(payload):
        sent = [lax.ppermute(payload[i : i + 1], "chan", p) for i, p in enumerate(moves)]
        return jnp.concatenate(sent)

    rims, keep = call(
        rim_kernel,
        [HBM, HBM],
        [((turns, RIM, n_rows, n_cols), bf16), ((chan_count + 2 * RIM, LANES), f32)],
        [
            SMEM((chan_count,), jnp.int32),
            VMEM((turns, RIM, n_rows, n_cols), bf16),
            dma((turns + 1,)),
        ],
        10**6,
    )(chan_flags, sky_cube)
    rim = across(rims)
    own, mid_band, edge_band, matrix = call(
        load_kernel,
        [HBM] * 4,
        [(v.shape, bf16) for v in (sky_cube, mid_band, edge_band, matrix)],
        [dma((4,))],
        10**6,
    )(sky_cube, mid_band, edge_band, matrix)

    mid_out = ((2, 2 * chan_count * mid, n_cols), f32)
    sums_out = ((slots, LANES), f32)
    spec, spec_squares, middle, middle_squares, sums = call(
        middle_kernel,
        [VMEM] * 5,
        [
            ((2, chan_count, n_rows, n_cols), bf16),
            ((2, chan_count, n_rows, n_cols), f32),
            mid_out,
            mid_out,
            sums_out,
        ],
        [VMEM(mid_out[0], bf16), VMEM((slots, 8, LANES), f32)],
        2 * 10**9,
    )(keep, own, rim, mid_band, matrix)

    (corners,) = call(
        corner_kernel, [VMEM] * 3, [((turns, 2 * RIM, EDGE, n_cols), bf16)], [], 10**6
    )(keep, first_pair, second_pair)
    corners = across(corners)

    def edge(pairs, rims, *args):
        count = turns * RIM if rims else chan_count - turns * RIM
        count *= len(pairs)
        outs = [((2, 2 * chan_count * EDGE, n_cols), f32)] * (2 * len(pairs))
        in_place = {len(args) - len(outs) + i: i for i in range(len(outs))}
        return call(
            functools.partial(edge_kernel, pairs, turns, rims),
            [VMEM] * len(args),
            outs + [((strips, width), f32) if rims else sums_out],
            [
                VMEM((2, 2 * count * EDGE, n_cols), bf16),
                VMEM((slots - 2 * chan_count, 8, LANES), f32),
                VMEM((2, count, EDGE + near, n_cols), bf16),
            ],
            10**9,
            aliases=in_place if rims else {},
        )(*args)

    shared_args = (spec, edge_band, matrix)
    *two, sums = edge((1,), False, keep, second_pair, *shared_args, sums)
    *one, sums = edge((0,), False, keep, first_pair, *shared_args, sums)
    args = (keep, first_pair, second_pair, corners, *shared_args, sums)
    edge_one, one_squares, edge_two, two_squares, shared = edge((0, 1), True, *args, *one, *two)

    shared = lax.all_to_all(shared, "strip", 0, 0, tiled=True)
    (shared,) = call(
        functools.partial(clip_kernel, pixels),
        [VMEM] * 5,
        [((strips, width), f32)],
        [VMEM((width, LANES), f32), VMEM((slots, 8, LANES), f32)],
        10**8,
    )(shared, spec_squares, middle_squares, one_squares, two_squares)
    shared = lax.all_to_all(shared, "strip", 0, 0, tiled=True)
    (out,) = call(
        functools.partial(ratio_kernel, pixels),
        [VMEM] * 6,
        [((chan_count, n_rows, n_cols), bf16)],
        [VMEM((width, LANES), f32), VMEM((chan_count, n_rows, n_cols), bf16), dma((4,))],
        10**8,
        HBM,
    )(keep, shared, spec, middle, edge_one, edge_two)
    return out


def solution(mesh):
    in_specs = (P("chan", "strip", "groups"), P("chan"))
    out_specs = P("chan", "strip", "groups")
    return jax.shard_map(shards, mesh=mesh, in_specs=in_specs, out_specs=out_specs, check_vma=False)
```

```python
import functools
import math

import jax
import jax.numpy as jnp
import numpy as np
from jax import lax
from jax.experimental import pallas as pl
from jax.experimental.pallas import tpu as pltpu
from jax.sharding import PartitionSpec as P

gauss_settings = ((5.0, 8), (10.0, 15))
epsilon = 1e-06
clip_level = 3.0
RIM = 3
REACH = 15
EDGE = 16
LANES = 128
BLOCK = 2 * LANES
VMEM, HBM, SMEM = pltpu.VMEM, pltpu.HBM, pltpu.SMEM
f32, bf16 = jnp.float32, jnp.bfloat16


def gauss_weights(fwhm, radius):
    offsets = np.arange(-REACH, REACH + 1)
    spread = fwhm / (2.0 * math.sqrt(2.0 * math.log(2.0)))
    weights = np.exp(-(offsets**2) / (2.0 * spread**2)) * (np.abs(offsets) <= radius)
    weights = weights / weights.sum()
    return weights.astype(np.float32)


def band(out_positions, in_positions):
    offset = np.asarray(in_positions)[None, :] - np.asarray(out_positions)[:, None]
    inside = np.abs(offset) <= REACH
    index = np.clip(offset + REACH, 0, 2 * REACH)
    return np.stack([np.where(inside, gauss_weights(*s)[index], 0.0) for s in gauss_settings])


def constant(matrix):
    return jnp.asarray(matrix.astype(np.float32)).astype(bf16)


def fold(values):
    rows, cols = values.shape
    total = None
    for r in range(0, rows, 8):
        for c in range(0, cols, LANES):
            part = values[r : r + 8, c : c + LANES]
            total = part if total is None else total + part
    return total


def wide(ref, row, rows=EDGE):
    return jnp.broadcast_to(ref[pl.ds(row, 1), :], (rows, LANES))


def towards(chan_count, turns):
    last = chan_count - RIM
    if turns == 1:
        return [jnp.where(lax.axis_index("chan") == 0, last, 0)]
    return [last, 0]


def rest(chan_count, turns):
    if turns == 1:
        return jnp.where(lax.axis_index("chan") == 0, 0, RIM), chan_count - RIM
    return RIM, chan_count - 2 * RIM


def pair_rows(n_rows, pair):
    odd = lax.rem(lax.axis_index("strip"), 2)
    at_end = odd == pair
    return pl.multiple_of(jnp.where(at_end, n_rows - EDGE, 0), EDGE)


def spectral_slot(chan_count, w, c):
    return w * chan_count + c


def smooth_slot(chan_count, w, f, c):
    return (2 + 2 * w + f) * chan_count + c


def means(x):
    for i in range(RIM, len(x) - RIM):
        s3 = x[i - 1] + x[i] + x[i + 1]
        s7 = (x[i - 3] + x[i - 2]) + s3 + (x[i + 2] + x[i + 3])
        yield i - RIM, [(s3 * (1.0 / 3.0)).astype(bf16), (s7 * (1.0 / 7.0)).astype(bf16)]


def row_pass(taps, plane, rowwise, slots, count, at=0):
    per = taps.shape[0] // 2
    for i in range(count):
        row = jnp.dot(taps, plane(slots[i]), preferred_element_type=f32).astype(bf16)
        start = (at + i) * per
        if not isinstance(start, int):
            start = pl.multiple_of(start, per)
        for f in range(2):
            rowwise[f, pl.ds(start, per), :] = row[f * per : (f + 1) * per]


def column_pass(rowwise, matrix, count, put):
    n_cols = rowwise.shape[2]
    per = rowwise.shape[1] // count
    blocks = n_cols // BLOCK
    for f in range(2):
        products = []
        for i in range(2 * blocks - 1):
            b = i * BLOCK if i < blocks else (i - blocks) * BLOCK + LANES
            x = rowwise[f, :, b : b + BLOCK]
            products.append(jnp.dot(x, matrix[f, i], preferred_element_type=f32))
        diagonal, seams = products[:blocks], products[blocks:]
        for slot in range(count):
            rows = slice(slot * per, (slot + 1) * per)
            values = []
            for l in range(0, n_cols, LANES):
                b, right = l // BLOCK, l % BLOCK
                value = diagonal[b][rows, right : right + LANES]
                if right and b < len(seams):
                    value = value + seams[b][rows, :LANES]
                if not right and b > 0:
                    value = value + seams[b - 1][rows, LANES:]
                values.append(value)
            put(f, slot, values)


def put_tiles(smooth, squares, acc, f, start, slot, values, add=False):
    rows = pl.ds(start, values[0].shape[0])
    total = None
    for i, value in enumerate(values):
        cols = slice(i * LANES, (i + 1) * LANES)
        square = value * value
        smooth[f, rows, cols] = value
        squares[f, rows, cols] = square
        part = fold(square)
        total = part if total is None else total + part
    acc[slot] = acc[slot] + total if add else total


def run(copies):
    for copy in copies:
        copy.start()
    for copy in copies:
        copy.wait()


def packed(chan_count):
    return chan_count - 1 if chan_count > REACH else chan_count


def spare_row(at_end):
    tile = pl.ds(pl.multiple_of(jnp.where(at_end, 0, EDGE - 8), 8), 8)
    return tile, jnp.where(at_end, 0, 7), jnp.where(at_end, 1, 0)


def pick_kernel(sky, first_pair, second_pair, last, lasts, sems):
    chan_count, n_rows, n_cols = sky.shape
    sent = packed(chan_count)
    pieces = (first_pair, second_pair)
    starts = [pair_rows(n_rows, pair) for pair in range(2)]
    copies = []
    for pair in range(2):
        rows = pl.ds(starts[pair], EDGE)
        source = sky.at[:sent, rows, :]
        copies.append(pltpu.make_async_copy(source, pieces[pair], sems.at[2 * pair]))
        if sent < chan_count:
            source = sky.at[sent, rows, :]
            copies.append(pltpu.make_async_copy(source, last.at[pair], sems.at[2 * pair + 1]))
    run(copies)
    if sent == chan_count:
        return
    row_index = lax.broadcasted_iota(jnp.int32, (8, n_cols), 0)
    for pair in range(2):
        tile, spare, first = spare_row(starts[pair] > 0)
        lasts[pair] = last[pair].astype(f32)
        for i in range(REACH):
            row = jnp.broadcast_to(lasts[pair, pl.ds(first + i, 1), :], (8, n_cols))
            value = pieces[pair][i, tile, :].astype(f32)
            value = jnp.where(row_index == spare, row, value)
            pieces[pair][i, tile, :] = value.astype(bf16)


def unpack(pair, n_rows, halo, last):
    tile, _, first = spare_row(pair_rows(n_rows, pair) == 0)
    last[...] = jnp.zeros_like(last)
    for i in range(REACH):
        value = halo[i, tile, :].astype(f32)
        last[pl.ds(first + i, 1), :] = jnp.where(first == 1, value[:1], value[7:])


def halo_tile(halo, last, c, cols, may_be_last):
    value = halo[jnp.clip(c, 0, halo.shape[0] - 1), :, cols].astype(f32)
    if may_be_last:
        value = jnp.where(c == halo.shape[0], last[:, cols], value)
    return value


def rim_kernel(flags, sky, rims, keep, flag, raw, sems):
    chan_count, _, _ = sky.shape
    turns = rims.shape[0]
    first = towards(chan_count, turns)
    copies = [pltpu.make_async_copy(flags, flag, sems.at[turns])]
    for turn in range(turns):
        source = sky.at[pl.ds(first[turn], RIM)]
        copies.append(pltpu.make_async_copy(source, raw.at[turn], sems.at[turn]))
    run(copies)
    block = lax.axis_index("chan")
    before = (block > 0).astype(jnp.int32)
    after = (block < lax.axis_size("chan") - 1).astype(jnp.int32)
    factors = [before] * RIM + [1 - flag[c] for c in range(chan_count)] + [after] * RIM
    for i, factor in enumerate(factors):
        keep[i : i + 1, :] = jnp.full((1, LANES), factor.astype(f32), f32)
    for turn in range(turns):
        for i in range(RIM):
            factor = (1 - flag[first[turn] + i]).astype(f32)
            rims[turn, i] = (raw[turn, i].astype(f32) * factor).astype(bf16)


def load_kernel(sky, mid_in, edge_in, matrix_in, own, mid_band, edge_band, matrix, sems):
    run(
        [
            pltpu.make_async_copy(sky, own, sems.at[0]),
            pltpu.make_async_copy(matrix_in, matrix, sems.at[1]),
            pltpu.make_async_copy(mid_in, mid_band, sems.at[2]),
            pltpu.make_async_copy(edge_in, edge_band, sems.at[3]),
        ]
    )


def corner_kernel(n_rows, keep, first_pair, second_pair, corners, lasts):
    n_cols = first_pair.shape[2]
    chan_count = keep.shape[0] - 2 * RIM
    split = first_pair.shape[0] < chan_count
    for pair, halo in enumerate((first_pair, second_pair)):
        last = lasts.at[pair]
        if split:
            unpack(pair, n_rows, halo, last)
        for turn, first in enumerate(towards(chan_count, corners.shape[0])):
            for i in range(RIM):
                factor = wide(keep, RIM + first + i)
                for l in range(0, n_cols, LANES):
                    cols = slice(l, l + LANES)
                    value = halo_tile(halo, last, first + i, cols, split and i == RIM - 1)
                    corners[turn, pair * RIM + i, :, cols] = (value * factor).astype(bf16)


def middle_kernel(
    keep, sky, rim, row_band, matrix, spec, spec_exact, spec_squares, smooth, squares, sums, rowwise, acc
):
    chan_count, n_rows, n_cols = sky.shape
    per = n_rows - 2 * EDGE

    @pl.loop(0, n_rows // EDGE)
    def _(t):
        rows = pl.ds(pl.multiple_of(t * EDGE, EDGE), EDGE)
        for lane in range(0, n_cols, LANES):
            cols = slice(lane, lane + LANES)
            x = [rim[0, i, rows, cols] for i in range(RIM)]
            x += [sky[c, rows, cols] for c in range(chan_count)]
            x += [rim[rim.shape[0] - 1, i, rows, cols] for i in range(RIM)]
            x = [value.astype(f32) * wide(keep, i) for i, value in enumerate(x)]
            for c, both in means(x):
                for w in range(2):
                    spec[w, c, rows, cols] = both[w]

    group = 4

    @pl.loop(0, chan_count // group)
    def _(g):
        for w in range(2):

            def plane(c):
                value = spec[w, c]
                exact = value.astype(f32)
                square = exact * exact
                spec_exact[w, c] = exact
                spec_squares[w, c] = square
                acc[spectral_slot(chan_count, w, c)] = fold(square)
                return value

            c = [g * group + i for i in range(group)]
            row_pass(row_band[...], plane, rowwise, c, group, w * chan_count + g * group)

    def put(f, slot, values):
        w, c = slot // chan_count, slot % chan_count
        target = smooth_slot(chan_count, w, f, c)
        put_tiles(smooth, squares, acc, f, slot * per, target, values)

    column_pass(rowwise, matrix, 2 * chan_count, put)
    sums[...] = jnp.sum(acc[...], axis=1)


def edge_kernel(pairs, turns, rims, *refs):
    refs = list(refs)

    def take(count):
        taken = refs[:count]
        del refs[:count]
        return taken

    (keep,) = take(1)
    halos = take(len(pairs))
    corners = take(1)[0] if rims else None
    spec, row_band, matrix, sums = take(4)
    if rims:
        take(2 * len(pairs))
    outs = [take(2) for _ in pairs]
    sums_out, rowwise, acc, frame, lasts = refs
    chan_count, n_rows, n_cols = spec.shape[1:]
    near = frame.shape[2] - EDGE
    groups = [rest(chan_count, turns) + (None,)]
    if rims:
        groups = [(first, RIM, turn) for turn, first in enumerate(towards(chan_count, turns))]

    planes, taps = [], []
    for side, pair in enumerate(pairs):
        at = pair_rows(n_rows, pair)
        inside = pl.multiple_of(jnp.where(at == 0, 0, n_rows - near), EDGE)
        taps.append(row_band[jnp.where(at == 0, 0, 1)])
        halo, last = halos[side], lasts.at[side]
        split = halo.shape[0] < chan_count
        if split:
            unpack(pair, n_rows, halo, last)
        for first, count, turn in groups:
            may_start = [0, RIM] if turn is None else [0, chan_count - RIM]
            base = len(planes)
            planes += [(side, first + i) for i in range(count)]
            for lane in range(0, n_cols, LANES):
                cols = slice(lane, lane + LANES)
                x = []
                for i in range(count + 2 * RIM):
                    c = first - RIM + i
                    may_be_last = split and chan_count - 1 + RIM - i in may_start
                    value = halo_tile(halo, last, c, cols, may_be_last)
                    if turn is not None and (i < RIM or i >= count + RIM):
                        at_rim = pair * RIM + (i if i < RIM else i - count - RIM)
                        other = corners[turns - 1 - turn, at_rim, :, cols]
                        own = jnp.logical_and(c >= 0, c < chan_count)
                        value = jnp.where(own, value, other.astype(f32))
                    x.append(value * wide(keep, RIM + c))
                for i, both in means(x):
                    for w in range(2):
                        frame[w, base + i, :EDGE, cols] = both[w]
            for w in range(2):
                inner = spec[w, pl.ds(first, count), pl.ds(inside, near), :]
                frame[w, base : base + count, EDGE:, :] = inner

    count = len(planes)
    each = count // len(pairs)
    for w in range(2):
        for side in range(len(pairs)):
            slots = list(range(side * each, (side + 1) * each))
            row_pass(taps[side], lambda i: frame[w, i], rowwise, slots, each, w * count + side * each)
    acc[...] = jnp.zeros_like(acc)

    def put(f, slot, values):
        w = slot // count
        side, c = planes[slot % count]
        start = pl.multiple_of((w * chan_count + c) * EDGE, EDGE)
        target = smooth_slot(chan_count, w, f, c) - 2 * chan_count
        put_tiles(*outs[side], acc, f, start, target, values, side > 0)

    column_pass(rowwise, matrix, 2 * count, put)
    before = sums[: 2 * chan_count, :]
    total = sums[2 * chan_count :, :] + jnp.sum(acc[...], axis=1)
    if rims:
        sums_out[...] = share(jnp.concatenate([before, total]), sums_out)
    else:
        sums_out[: 2 * chan_count, :] = before
        sums_out[2 * chan_count :, :] = total


def share(acc_sum, out):
    peers, width = out.shape
    slots = acc_sum.shape[0]
    if slots < width:
        acc_sum = jnp.concatenate([acc_sum, jnp.zeros((width - slots, LANES), f32)], axis=0)
    total = jnp.sum(acc_sum.T, axis=0, keepdims=True)
    return jnp.broadcast_to(total, (peers, width))


def spread(shared):
    total = jnp.sum(shared[...], axis=0, keepdims=True)
    return jnp.broadcast_to(total, (LANES, total.shape[1])).T


def clip_kernel(pixels, shared_in, spec, middle, edge_one, edge_two, shared, limit, acc):
    chan_count = spec.shape[1]
    rough = jnp.sqrt(spread(shared_in) / pixels + epsilon)
    limit[...] = (clip_level * rough) ** 2

    @pl.loop(0, chan_count)
    def _(c):
        def clipped(slot, parts):
            top = wide(limit, slot, 8)
            total = None
            for part in parts:
                for r in range(0, part.shape[0], 8):
                    for l in range(0, part.shape[1], LANES):
                        value = jnp.minimum(part[r : r + 8, l : l + LANES], top)
                        total = value if total is None else total + value
            acc[slot] = total

        for w in range(2):
            clipped(spectral_slot(chan_count, w, c), [spec[w, c]])
            for f in range(2):
                parts = []
                for source in (middle, edge_one, edge_two):
                    per = source.shape[1] // (2 * chan_count)
                    start = pl.multiple_of((w * chan_count + c) * per, per)
                    parts.append(source[f, pl.ds(start, per), :])
                clipped(smooth_slot(chan_count, w, f, c), parts)

    shared[...] = share(jnp.sum(acc[...], axis=1), shared)


def ratio_kernel(pixels, keep, shared_in, spec, middle, edge_one, edge_two, out, scale, staged, sems):
    chan_count, n_rows, n_cols = out.shape
    scale[...] = 1.0 / jnp.sqrt(spread(shared_in) / pixels + epsilon)
    for k in range(6):
        rows = slice(k * chan_count, (k + 1) * chan_count)
        scale[rows, :] = scale[rows, :] * keep[RIM : RIM + chan_count, :]
    parts = sems.shape[0]
    group = chan_count // parts
    tiles = [(middle, r, EDGE + r) for r in range(0, n_rows - 2 * EDGE, EDGE)]
    tiles += [(edge_one, 0, pair_rows(n_rows, 0)), (edge_two, 0, pair_rows(n_rows, 1))]

    def channel(c):
        factors = [
            [wide(scale, spectral_slot(chan_count, w, c))]
            + [wide(scale, smooth_slot(chan_count, w, f, c)) for f in range(2)]
            for w in range(2)
        ]
        for source, offset, row in tiles:
            rows = pl.ds(row, EDGE)
            per = source.shape[1] // (2 * chan_count)
            for l in range(0, n_cols, LANES):
                cols = slice(l, l + LANES)
                best = None
                for w in range(2):
                    start = pl.multiple_of((w * chan_count + c) * per + offset, EDGE)
                    values = [spec[w, c, rows, cols]]
                    values += [source[f, pl.ds(start, EDGE), cols] for f in range(2)]
                    for value, factor in zip(values, factors[w]):
                        value = value * factor
                        best = value if best is None else jnp.maximum(best, value)
                staged[c, rows, cols] = best.astype(bf16)

    copies = []
    for p in range(parts):
        pl.loop(p * group, (p + 1) * group)(channel)
        s = slice(p * group, (p + 1) * group)
        copies.append(pltpu.make_async_copy(staged.at[s], out.at[s], sems.at[p]))
        copies[-1].start()
    for copy in copies:
        copy.wait()


def specs(spaces):
    return [pl.BlockSpec(memory_space=s) for s in spaces]


def call(kernel, ins, outs, scratch, flops, out_space=VMEM, aliases={}):
    return pl.pallas_call(
        kernel,
        in_specs=specs(ins),
        out_specs=specs([out_space] * len(outs)),
        out_shape=[jax.ShapeDtypeStruct(s, d) for s, d in outs],
        scratch_shapes=scratch,
        input_output_aliases=aliases,
        compiler_params=pltpu.CompilerParams(vmem_limit_bytes=12 * 2**20),
        cost_estimate=pl.CostEstimate(flops=flops, bytes_accessed=2**20, transcendentals=0),
    )


def shards(sky_cube, chan_flags):
    chan_count, n_rows, n_cols = sky_cube.shape
    strips, blocks = lax.axis_size("strip"), lax.axis_size("chan")
    pixels = n_rows * strips * n_cols
    turns = 1 if blocks == 2 else 2
    slots = 6 * chan_count
    width = -(-slots // LANES) * LANES
    mid = n_rows - 2 * EDGE
    near = 2 * EDGE
    dma = pltpu.SemaphoreType.DMA

    own_rows = np.arange(n_rows)
    mid_band = constant(band(own_rows[EDGE : n_rows - EDGE], own_rows).reshape(2 * mid, n_rows))
    top = band(np.arange(EDGE), np.concatenate([np.arange(-EDGE, 0), np.arange(near)]))
    bottom = band(np.arange(near - EDGE, near), np.concatenate([np.arange(near, near + EDGE), np.arange(near)]))
    edge_band = constant(np.stack([top, bottom]).reshape(2, 2 * EDGE, EDGE + near))
    cols = np.arange(n_cols)
    taps = band(cols, cols).transpose(0, 2, 1)
    same = cols[:, None] // BLOCK == cols[None, :] // BLOCK
    starts = np.arange(0, n_cols, BLOCK)
    pieces = [(taps * same)[:, b : b + BLOCK, b : b + BLOCK] for b in starts]
    pieces += [(taps * ~same)[:, b : b + BLOCK, b : b + BLOCK] for b in starts[:-1] + LANES]
    matrix = constant(np.stack(pieces, axis=1))

    sky_cube, chan_flags, mid_band, edge_band, matrix = (
        pltpu.with_memory_space_constraint(v, HBM)
        for v in (sky_cube, chan_flags, mid_band, edge_band, matrix)
    )

    edge_rows = ((packed(chan_count), EDGE, n_cols), bf16)
    last_rows = (2, EDGE, n_cols)
    first_pair, second_pair = call(
        pick_kernel,
        [HBM],
        [edge_rows, edge_rows],
        [VMEM(last_rows, bf16), VMEM(last_rows, f32), dma((4,))],
        10**6,
    )(sky_cube)

    evens = [(i, i + 1) for i in range(0, strips - 1, 2)]
    odds = [(i, i + 1) for i in range(1, strips - 1, 2)]
    evens, odds = (p + [(b, a) for a, b in p] for p in (evens, odds))
    first_pair = lax.ppermute(first_pair, "strip", evens)
    second_pair = lax.ppermute(second_pair, "strip", odds)

    forth = [(i, i + 1) for i in range(blocks - 1)]
    back = [(j, i) for i, j in forth]
    moves = [forth + back] if turns == 1 else [forth, back]

    def across(payload):
        sent = [lax.ppermute(payload[i : i + 1], "chan", p) for i, p in enumerate(moves)]
        return jnp.concatenate(sent)

    rims, keep = call(
        rim_kernel,
        [HBM, HBM],
        [((turns, RIM, n_rows, n_cols), bf16), ((chan_count + 2 * RIM, LANES), f32)],
        [
            SMEM((chan_count,), jnp.int32),
            VMEM((turns, RIM, n_rows, n_cols), bf16),
            dma((turns + 1,)),
        ],
        10**6,
    )(chan_flags, sky_cube)
    rim = across(rims)
    own, mid_band, edge_band, matrix = call(
        load_kernel,
        [HBM] * 4,
        [(v.shape, bf16) for v in (sky_cube, mid_band, edge_band, matrix)],
        [dma((4,))],
        10**6,
    )(sky_cube, mid_band, edge_band, matrix)

    mid_out = ((2, 2 * chan_count * mid, n_cols), f32)
    sums_out = ((slots, LANES), f32)
    spec, spec_exact, spec_squares, middle, middle_squares, sums = call(
        middle_kernel,
        [VMEM] * 5,
        [
            ((2, chan_count, n_rows, n_cols), bf16),
            ((2, chan_count, n_rows, n_cols), f32),
            ((2, chan_count, n_rows, n_cols), f32),
            mid_out,
            mid_out,
            sums_out,
        ],
        [VMEM(mid_out[0], bf16), VMEM((slots, 8, LANES), f32)],
        2 * 10**9,
    )(keep, own, rim, mid_band, matrix)

    (corners,) = call(
        functools.partial(corner_kernel, n_rows),
        [VMEM] * 3,
        [((turns, 2 * RIM, EDGE, n_cols), bf16)],
        [VMEM(last_rows, f32)],
        10**6,
    )(keep, first_pair, second_pair)
    corners = across(corners)

    def edge(pairs, rims, *args):
        count = turns * RIM if rims else chan_count - turns * RIM
        count *= len(pairs)
        outs = [((2, 2 * chan_count * EDGE, n_cols), f32)] * (2 * len(pairs))
        in_place = {len(args) - len(outs) + i: i for i in range(len(outs))}
        return call(
            functools.partial(edge_kernel, pairs, turns, rims),
            [VMEM] * len(args),
            outs + [((strips, width), f32) if rims else sums_out],
            [
                VMEM((2, 2 * count * EDGE, n_cols), bf16),
                VMEM((slots - 2 * chan_count, 8, LANES), f32),
                VMEM((2, count, EDGE + near, n_cols), bf16),
                VMEM((len(pairs), EDGE, n_cols), f32),
            ],
            10**9,
            aliases=in_place if rims else {},
        )(*args)

    shared_args = (spec, edge_band, matrix)
    *two, sums = edge((1,), False, keep, second_pair, *shared_args, sums)
    *one, sums = edge((0,), False, keep, first_pair, *shared_args, sums)
    args = (keep, first_pair, second_pair, corners, *shared_args, sums)
    edge_one, one_squares, edge_two, two_squares, shared = edge((0, 1), True, *args, *one, *two)

    shared = lax.all_to_all(shared, "strip", 0, 0, tiled=True)
    (shared,) = call(
        functools.partial(clip_kernel, pixels),
        [VMEM] * 5,
        [((strips, width), f32)],
        [VMEM((width, LANES), f32), VMEM((slots, 8, LANES), f32)],
        10**8,
    )(shared, spec_squares, middle_squares, one_squares, two_squares)
    shared = lax.all_to_all(shared, "strip", 0, 0, tiled=True)
    (out,) = call(
        functools.partial(ratio_kernel, pixels),
        [VMEM] * 6,
        [((chan_count, n_rows, n_cols), bf16)],
        [VMEM((width, LANES), f32), VMEM((chan_count, n_rows, n_cols), bf16), dma((4,))],
        10**8,
        HBM,
    )(keep, shared, spec_exact, middle, edge_one, edge_two)
    return out


def solution(mesh):
    in_specs = (P("chan", "strip", "groups"), P("chan"))
    out_specs = P("chan", "strip", "groups")
    return jax.shard_map(shards, mesh=mesh, in_specs=in_specs, out_specs=out_specs, check_vma=False)
```

```python
import functools
import math

import jax
import jax.numpy as jnp
import numpy as np
from jax import lax
from jax.experimental import pallas as pl
from jax.experimental.pallas import tpu as pltpu
from jax.sharding import PartitionSpec as P

gauss_settings = ((5.0, 8), (10.0, 15))
epsilon = 1e-06
clip_level = 3.0
RIM = 3
REACH = 15
EDGE = 16
LANES = 128
BLOCK = 2 * LANES
VMEM, HBM, SMEM = pltpu.VMEM, pltpu.HBM, pltpu.SMEM
f32, bf16 = jnp.float32, jnp.bfloat16


def gauss_weights(fwhm, radius):
    offsets = np.arange(-REACH, REACH + 1)
    spread = fwhm / (2.0 * math.sqrt(2.0 * math.log(2.0)))
    weights = np.exp(-(offsets**2) / (2.0 * spread**2)) * (np.abs(offsets) <= radius)
    weights = weights / weights.sum()
    return weights.astype(np.float32)


def band(out_positions, in_positions):
    offset = np.asarray(in_positions)[None, :] - np.asarray(out_positions)[:, None]
    inside = np.abs(offset) <= REACH
    index = np.clip(offset + REACH, 0, 2 * REACH)
    return np.stack([np.where(inside, gauss_weights(*s)[index], 0.0) for s in gauss_settings])


def constant(matrix):
    return jnp.asarray(matrix.astype(np.float32)).astype(bf16)


def fold(values):
    rows, cols = values.shape
    total = None
    for r in range(0, rows, 8):
        for c in range(0, cols, LANES):
            part = values[r : r + 8, c : c + LANES]
            total = part if total is None else total + part
    return total


def wide(ref, row, rows=EDGE):
    return jnp.broadcast_to(ref[pl.ds(row, 1), :], (rows, LANES))


def towards(chan_count, turns):
    last = chan_count - RIM
    if turns == 1:
        return [jnp.where(lax.axis_index("chan") == 0, last, 0)]
    return [last, 0]


def rest(chan_count, turns):
    if turns == 1:
        return jnp.where(lax.axis_index("chan") == 0, 0, RIM), chan_count - RIM
    return RIM, chan_count - 2 * RIM


def pair_rows(n_rows, pair):
    odd = lax.rem(lax.axis_index("strip"), 2)
    at_end = odd == pair
    return pl.multiple_of(jnp.where(at_end, n_rows - EDGE, 0), EDGE)


def spectral_slot(chan_count, w, c):
    return w * chan_count + c


def smooth_slot(chan_count, w, f, c):
    return (2 + 2 * w + f) * chan_count + c


def means(x):
    for i in range(RIM, len(x) - RIM):
        s3 = x[i - 1] + x[i] + x[i + 1]
        s7 = (x[i - 3] + x[i - 2]) + s3 + (x[i + 2] + x[i + 3])
        yield i - RIM, [(s3 * (1.0 / 3.0)).astype(bf16), (s7 * (1.0 / 7.0)).astype(bf16)]


def row_pass(taps, plane, rowwise, slots, count, at=0):
    per = taps.shape[0] // 2
    for i in range(count):
        row = jnp.dot(taps, plane(slots[i]), preferred_element_type=f32).astype(bf16)
        start = (at + i) * per
        if not isinstance(start, int):
            start = pl.multiple_of(start, per)
        for f in range(2):
            rowwise[f, pl.ds(start, per), :] = row[f * per : (f + 1) * per]


def column_pass(rowwise, matrix, count, put):
    n_cols = rowwise.shape[2]
    per = rowwise.shape[1] // count
    blocks = n_cols // BLOCK
    for f in range(2):
        products = []
        for i in range(2 * blocks - 1):
            b = i * BLOCK if i < blocks else (i - blocks) * BLOCK + LANES
            x = rowwise[f, :, b : b + BLOCK]
            products.append(jnp.dot(x, matrix[f, i], preferred_element_type=f32))
        diagonal, seams = products[:blocks], products[blocks:]
        for slot in range(count):
            rows = slice(slot * per, (slot + 1) * per)
            values = []
            for l in range(0, n_cols, LANES):
                b, right = l // BLOCK, l % BLOCK
                value = diagonal[b][rows, right : right + LANES]
                if right and b < len(seams):
                    value = value + seams[b][rows, :LANES]
                if not right and b > 0:
                    value = value + seams[b - 1][rows, LANES:]
                values.append(value)
            put(f, slot, values)


def put_tiles(smooth, squares, acc, f, start, slot, values, add=False):
    rows = pl.ds(start, values[0].shape[0])
    total = None
    for i, value in enumerate(values):
        cols = slice(i * LANES, (i + 1) * LANES)
        square = value * value
        smooth[f, rows, cols] = value
        squares[f, rows, cols] = square
        part = fold(square)
        total = part if total is None else total + part
    acc[slot] = acc[slot] + total if add else total


def run(copies):
    for copy in copies:
        copy.start()
    for copy in copies:
        copy.wait()


def packed(chan_count):
    return chan_count - 1 if chan_count > REACH else chan_count


def spare_row(at_end):
    tile = pl.ds(pl.multiple_of(jnp.where(at_end, 0, EDGE - 8), 8), 8)
    return tile, jnp.where(at_end, 0, 7), jnp.where(at_end, 1, 0)


def pick_kernel(sky, first_pair, second_pair, last, lasts, sems):
    chan_count, n_rows, n_cols = sky.shape
    sent = packed(chan_count)
    pieces = (first_pair, second_pair)
    starts = [pair_rows(n_rows, pair) for pair in range(2)]
    copies = []
    for pair in range(2):
        rows = pl.ds(starts[pair], EDGE)
        source = sky.at[:sent, rows, :]
        copies.append(pltpu.make_async_copy(source, pieces[pair], sems.at[2 * pair]))
        if sent < chan_count:
            source = sky.at[sent, rows, :]
            copies.append(pltpu.make_async_copy(source, last.at[pair], sems.at[2 * pair + 1]))
    run(copies)
    if sent == chan_count:
        return
    row_index = lax.broadcasted_iota(jnp.int32, (8, n_cols), 0)
    for pair in range(2):
        tile, spare, first = spare_row(starts[pair] > 0)
        lasts[pair] = last[pair].astype(f32)
        for i in range(REACH):
            row = jnp.broadcast_to(lasts[pair, pl.ds(first + i, 1), :], (8, n_cols))
            value = pieces[pair][i, tile, :].astype(f32)
            value = jnp.where(row_index == spare, row, value)
            pieces[pair][i, tile, :] = value.astype(bf16)


def unpack(pair, n_rows, halo, last):
    tile, _, first = spare_row(pair_rows(n_rows, pair) == 0)
    last[...] = jnp.zeros_like(last)
    for i in range(REACH):
        value = halo[i, tile, :].astype(f32)
        last[pl.ds(first + i, 1), :] = jnp.where(first == 1, value[:1], value[7:])


def halo_tile(halo, last, c, cols, may_be_last):
    value = halo[jnp.clip(c, 0, halo.shape[0] - 1), :, cols].astype(f32)
    if may_be_last:
        value = jnp.where(c == halo.shape[0], last[:, cols], value)
    return value


def rim_kernel(flags, sky, rims, keep, flag, raw, sems):
    chan_count, _, _ = sky.shape
    turns = rims.shape[0]
    first = towards(chan_count, turns)
    copies = [pltpu.make_async_copy(flags, flag, sems.at[turns])]
    for turn in range(turns):
        source = sky.at[pl.ds(first[turn], RIM)]
        copies.append(pltpu.make_async_copy(source, raw.at[turn], sems.at[turn]))
    run(copies)
    block = lax.axis_index("chan")
    before = (block > 0).astype(jnp.int32)
    after = (block < lax.axis_size("chan") - 1).astype(jnp.int32)
    factors = [before] * RIM + [1 - flag[c] for c in range(chan_count)] + [after] * RIM
    for i, factor in enumerate(factors):
        keep[i : i + 1, :] = jnp.full((1, LANES), factor.astype(f32), f32)
    for turn in range(turns):
        for i in range(RIM):
            factor = (1 - flag[first[turn] + i]).astype(f32)
            rims[turn, i] = (raw[turn, i].astype(f32) * factor).astype(bf16)


def load_kernel(sky, mid_in, edge_in, matrix_in, own, mid_band, edge_band, matrix, sems):
    run(
        [
            pltpu.make_async_copy(sky, own, sems.at[0]),
            pltpu.make_async_copy(matrix_in, matrix, sems.at[1]),
            pltpu.make_async_copy(mid_in, mid_band, sems.at[2]),
            pltpu.make_async_copy(edge_in, edge_band, sems.at[3]),
        ]
    )


def corner_kernel(n_rows, keep, first_pair, second_pair, corners, lasts):
    n_cols = first_pair.shape[2]
    chan_count = keep.shape[0] - 2 * RIM
    split = first_pair.shape[0] < chan_count
    for pair, halo in enumerate((first_pair, second_pair)):
        last = lasts.at[pair]
        if split:
            unpack(pair, n_rows, halo, last)
        for turn, first in enumerate(towards(chan_count, corners.shape[0])):
            for i in range(RIM):
                factor = wide(keep, RIM + first + i)
                for l in range(0, n_cols, LANES):
                    cols = slice(l, l + LANES)
                    value = halo_tile(halo, last, first + i, cols, split and i == RIM - 1)
                    corners[turn, pair * RIM + i, :, cols] = (value * factor).astype(bf16)


def middle_kernel(
    keep, sky, rim, row_band, matrix, spec, spec_exact, spec_squares, smooth, squares, sums, rowwise, acc
):
    chan_count, n_rows, n_cols = sky.shape
    per = n_rows - 2 * EDGE

    @pl.loop(0, n_rows // EDGE)
    def _(t):
        rows = pl.ds(pl.multiple_of(t * EDGE, EDGE), EDGE)
        for lane in range(0, n_cols, LANES):
            cols = slice(lane, lane + LANES)
            x = [rim[0, i, rows, cols] for i in range(RIM)]
            x += [sky[c, rows, cols] for c in range(chan_count)]
            x += [rim[rim.shape[0] - 1, i, rows, cols] for i in range(RIM)]
            x = [value.astype(f32) * wide(keep, i) for i, value in enumerate(x)]
            for c, both in means(x):
                for w in range(2):
                    spec[w, c, rows, cols] = both[w]

    group = 4

    @pl.loop(0, chan_count // group)
    def _(g):
        for w in range(2):

            def plane(c):
                value = spec[w, c]
                exact = value.astype(f32)
                square = exact * exact
                spec_exact[w, c] = exact
                spec_squares[w, c] = square
                acc[spectral_slot(chan_count, w, c)] = fold(square)
                return value

            c = [g * group + i for i in range(group)]
            row_pass(row_band[...], plane, rowwise, c, group, w * chan_count + g * group)

    def put(f, slot, values):
        w, c = slot // chan_count, slot % chan_count
        target = smooth_slot(chan_count, w, f, c)
        put_tiles(smooth, squares, acc, f, slot * per, target, values)

    column_pass(rowwise, matrix, 2 * chan_count, put)
    sums[...] = jnp.sum(acc[...], axis=1)


def edge_kernel(pairs, turns, rims, given, *refs):
    refs = list(refs)

    def take(count):
        taken = refs[:count]
        del refs[:count]
        return taken

    (keep,) = take(1)
    halos = take(len(pairs))
    corners = take(1)[0] if rims else None
    lasts = take(1)[0] if given else None
    spec, row_band, matrix, sums = take(4)
    if rims:
        take(2 * len(pairs))
    outs = [take(2) for _ in pairs]
    if lasts is None:
        lasts = refs.pop()
        unpacked = False
    else:
        unpacked = True
    sums_out, rowwise, acc, frame = refs
    chan_count, n_rows, n_cols = spec.shape[1:]
    near = frame.shape[2] - EDGE
    groups = [rest(chan_count, turns) + (None,)]
    if rims:
        groups = [(first, RIM, turn) for turn, first in enumerate(towards(chan_count, turns))]

    planes, taps = [], []
    for side, pair in enumerate(pairs):
        at = pair_rows(n_rows, pair)
        inside = pl.multiple_of(jnp.where(at == 0, 0, n_rows - near), EDGE)
        taps.append(row_band[jnp.where(at == 0, 0, 1)])
        halo, last = halos[side], lasts.at[pair if unpacked else side]
        split = halo.shape[0] < chan_count
        if split and not unpacked:
            unpack(pair, n_rows, halo, last)
        for first, count, turn in groups:
            may_start = [0, RIM] if turn is None else [0, chan_count - RIM]
            base = len(planes)
            planes += [(side, first + i) for i in range(count)]
            for lane in range(0, n_cols, LANES):
                cols = slice(lane, lane + LANES)
                x = []
                for i in range(count + 2 * RIM):
                    c = first - RIM + i
                    may_be_last = split and chan_count - 1 + RIM - i in may_start
                    value = halo_tile(halo, last, c, cols, may_be_last)
                    if turn is not None and (i < RIM or i >= count + RIM):
                        at_rim = pair * RIM + (i if i < RIM else i - count - RIM)
                        other = corners[turns - 1 - turn, at_rim, :, cols]
                        own = jnp.logical_and(c >= 0, c < chan_count)
                        value = jnp.where(own, value, other.astype(f32))
                    x.append(value * wide(keep, RIM + c))
                for i, both in means(x):
                    for w in range(2):
                        frame[w, base + i, :EDGE, cols] = both[w]
            for w in range(2):
                inner = spec[w, pl.ds(first, count), pl.ds(inside, near), :]
                frame[w, base : base + count, EDGE:, :] = inner

    count = len(planes)
    each = count // len(pairs)
    for w in range(2):
        for side in range(len(pairs)):
            slots = list(range(side * each, (side + 1) * each))
            row_pass(taps[side], lambda i: frame[w, i], rowwise, slots, each, w * count + side * each)
    acc[...] = jnp.zeros_like(acc)

    def put(f, slot, values):
        w = slot // count
        side, c = planes[slot % count]
        start = pl.multiple_of((w * chan_count + c) * EDGE, EDGE)
        target = smooth_slot(chan_count, w, f, c) - 2 * chan_count
        put_tiles(*outs[side], acc, f, start, target, values, side > 0)

    column_pass(rowwise, matrix, 2 * count, put)
    before = sums[: 2 * chan_count, :]
    total = sums[2 * chan_count :, :] + jnp.sum(acc[...], axis=1)
    if rims:
        sums_out[...] = share(jnp.concatenate([before, total]), sums_out)
    else:
        sums_out[: 2 * chan_count, :] = before
        sums_out[2 * chan_count :, :] = total


def share(acc_sum, out):
    peers, width = out.shape
    slots = acc_sum.shape[0]
    if slots < width:
        acc_sum = jnp.concatenate([acc_sum, jnp.zeros((width - slots, LANES), f32)], axis=0)
    total = jnp.sum(acc_sum.T, axis=0, keepdims=True)
    return jnp.broadcast_to(total, (peers, width))


def spread(shared):
    total = jnp.sum(shared[...], axis=0, keepdims=True)
    return jnp.broadcast_to(total, (LANES, total.shape[1])).T


def clip_kernel(pixels, shared_in, spec, middle, edge_one, edge_two, shared, limit, acc):
    chan_count = spec.shape[1]
    rough = jnp.sqrt(spread(shared_in) / pixels + epsilon)
    limit[...] = (clip_level * rough) ** 2

    @pl.loop(0, chan_count)
    def _(c):
        def clipped(slot, parts):
            top = wide(limit, slot, 8)
            total = None
            for part in parts:
                for r in range(0, part.shape[0], 8):
                    for l in range(0, part.shape[1], LANES):
                        value = jnp.minimum(part[r : r + 8, l : l + LANES], top)
                        total = value if total is None else total + value
            acc[slot] = total

        for w in range(2):
            clipped(spectral_slot(chan_count, w, c), [spec[w, c]])
            for f in range(2):
                parts = []
                for source in (middle, edge_one, edge_two):
                    per = source.shape[1] // (2 * chan_count)
                    start = pl.multiple_of((w * chan_count + c) * per, per)
                    parts.append(source[f, pl.ds(start, per), :])
                clipped(smooth_slot(chan_count, w, f, c), parts)

    shared[...] = share(jnp.sum(acc[...], axis=1), shared)


def ratio_kernel(pixels, keep, shared_in, spec, middle, edge_one, edge_two, out, scale, staged, sems):
    chan_count, n_rows, n_cols = out.shape
    scale[...] = 1.0 / jnp.sqrt(spread(shared_in) / pixels + epsilon)
    for k in range(6):
        rows = slice(k * chan_count, (k + 1) * chan_count)
        scale[rows, :] = scale[rows, :] * keep[RIM : RIM + chan_count, :]
    parts = sems.shape[0]
    group = chan_count // parts
    tiles = [(middle, r, EDGE + r) for r in range(0, n_rows - 2 * EDGE, EDGE)]
    tiles += [(edge_one, 0, pair_rows(n_rows, 0)), (edge_two, 0, pair_rows(n_rows, 1))]

    def channel(c):
        factors = [
            [wide(scale, spectral_slot(chan_count, w, c))]
            + [wide(scale, smooth_slot(chan_count, w, f, c)) for f in range(2)]
            for w in range(2)
        ]
        for source, offset, row in tiles:
            rows = pl.ds(row, EDGE)
            per = source.shape[1] // (2 * chan_count)
            for l in range(0, n_cols, LANES):
                cols = slice(l, l + LANES)
                best = None
                for w in range(2):
                    start = pl.multiple_of((w * chan_count + c) * per + offset, EDGE)
                    values = [spec[w, c, rows, cols]]
                    values += [source[f, pl.ds(start, EDGE), cols] for f in range(2)]
                    for value, factor in zip(values, factors[w]):
                        value = value * factor
                        best = value if best is None else jnp.maximum(best, value)
                staged[c, rows, cols] = best.astype(bf16)

    copies = []
    for p in range(parts):
        pl.loop(p * group, (p + 1) * group)(channel)
        s = slice(p * group, (p + 1) * group)
        copies.append(pltpu.make_async_copy(staged.at[s], out.at[s], sems.at[p]))
        copies[-1].start()
    for copy in copies:
        copy.wait()


def specs(spaces):
    return [pl.BlockSpec(memory_space=s) for s in spaces]


def call(kernel, ins, outs, scratch, flops, out_space=VMEM, aliases={}):
    return pl.pallas_call(
        kernel,
        in_specs=specs(ins),
        out_specs=specs([out_space] * len(outs)),
        out_shape=[jax.ShapeDtypeStruct(s, d) for s, d in outs],
        scratch_shapes=scratch,
        input_output_aliases=aliases,
        compiler_params=pltpu.CompilerParams(vmem_limit_bytes=12 * 2**20),
        cost_estimate=pl.CostEstimate(flops=flops, bytes_accessed=2**20, transcendentals=0),
    )


def shards(sky_cube, chan_flags):
    chan_count, n_rows, n_cols = sky_cube.shape
    strips, blocks = lax.axis_size("strip"), lax.axis_size("chan")
    pixels = n_rows * strips * n_cols
    turns = 1 if blocks == 2 else 2
    slots = 6 * chan_count
    width = -(-slots // LANES) * LANES
    mid = n_rows - 2 * EDGE
    near = 2 * EDGE
    dma = pltpu.SemaphoreType.DMA

    own_rows = np.arange(n_rows)
    mid_band = constant(band(own_rows[EDGE : n_rows - EDGE], own_rows).reshape(2 * mid, n_rows))
    top = band(np.arange(EDGE), np.concatenate([np.arange(-EDGE, 0), np.arange(near)]))
    bottom = band(np.arange(near - EDGE, near), np.concatenate([np.arange(near, near + EDGE), np.arange(near)]))
    edge_band = constant(np.stack([top, bottom]).reshape(2, 2 * EDGE, EDGE + near))
    cols = np.arange(n_cols)
    taps = band(cols, cols).transpose(0, 2, 1)
    same = cols[:, None] // BLOCK == cols[None, :] // BLOCK
    starts = np.arange(0, n_cols, BLOCK)
    pieces = [(taps * same)[:, b : b + BLOCK, b : b + BLOCK] for b in starts]
    pieces += [(taps * ~same)[:, b : b + BLOCK, b : b + BLOCK] for b in starts[:-1] + LANES]
    matrix = constant(np.stack(pieces, axis=1))

    sky_cube, chan_flags, mid_band, edge_band, matrix = (
        pltpu.with_memory_space_constraint(v, HBM)
        for v in (sky_cube, chan_flags, mid_band, edge_band, matrix)
    )

    edge_rows = ((packed(chan_count), EDGE, n_cols), bf16)
    last_rows = (2, EDGE, n_cols)
    first_pair, second_pair = call(
        pick_kernel,
        [HBM],
        [edge_rows, edge_rows],
        [VMEM(last_rows, bf16), VMEM(last_rows, f32), dma((4,))],
        10**6,
    )(sky_cube)

    evens = [(i, i + 1) for i in range(0, strips - 1, 2)]
    odds = [(i, i + 1) for i in range(1, strips - 1, 2)]
    evens, odds = (p + [(b, a) for a, b in p] for p in (evens, odds))
    first_pair = lax.ppermute(first_pair, "strip", evens)
    second_pair = lax.ppermute(second_pair, "strip", odds)

    forth = [(i, i + 1) for i in range(blocks - 1)]
    back = [(j, i) for i, j in forth]
    moves = [forth + back] if turns == 1 else [forth, back]

    def across(payload):
        sent = [lax.ppermute(payload[i : i + 1], "chan", p) for i, p in enumerate(moves)]
        return jnp.concatenate(sent)

    rims, keep = call(
        rim_kernel,
        [HBM, HBM],
        [((turns, RIM, n_rows, n_cols), bf16), ((chan_count + 2 * RIM, LANES), f32)],
        [
            SMEM((chan_count,), jnp.int32),
            VMEM((turns, RIM, n_rows, n_cols), bf16),
            dma((turns + 1,)),
        ],
        10**6,
    )(chan_flags, sky_cube)
    rim = across(rims)
    own, mid_band, edge_band, matrix = call(
        load_kernel,
        [HBM] * 4,
        [(v.shape, bf16) for v in (sky_cube, mid_band, edge_band, matrix)],
        [dma((4,))],
        10**6,
    )(sky_cube, mid_band, edge_band, matrix)

    mid_out = ((2, 2 * chan_count * mid, n_cols), f32)
    sums_out = ((slots, LANES), f32)
    spec, spec_exact, spec_squares, middle, middle_squares, sums = call(
        middle_kernel,
        [VMEM] * 5,
        [
            ((2, chan_count, n_rows, n_cols), bf16),
            ((2, chan_count, n_rows, n_cols), f32),
            ((2, chan_count, n_rows, n_cols), f32),
            mid_out,
            mid_out,
            sums_out,
        ],
        [VMEM(mid_out[0], bf16), VMEM((slots, 8, LANES), f32)],
        2 * 10**9,
    )(keep, own, rim, mid_band, matrix)

    corners, lasts = call(
        functools.partial(corner_kernel, n_rows),
        [VMEM] * 3,
        [((turns, 2 * RIM, EDGE, n_cols), bf16), (last_rows, f32)],
        [],
        10**6,
    )(keep, first_pair, second_pair)
    corners = across(corners)

    def edge(pairs, rims, given, *args):
        count = turns * RIM if rims else chan_count - turns * RIM
        count *= len(pairs)
        outs = [((2, 2 * chan_count * EDGE, n_cols), f32)] * (2 * len(pairs))
        in_place = {len(args) - len(outs) + i: i for i in range(len(outs))}
        return call(
            functools.partial(edge_kernel, pairs, turns, rims, given),
            [VMEM] * len(args),
            outs + [((strips, width), f32) if rims else sums_out],
            [
                VMEM((2, 2 * count * EDGE, n_cols), bf16),
                VMEM((slots - 2 * chan_count, 8, LANES), f32),
                VMEM((2, count, EDGE + near, n_cols), bf16),
            ]
            + ([] if given else [VMEM((len(pairs), EDGE, n_cols), f32)]),
            10**9,
            aliases=in_place if rims else {},
        )(*args)

    shared_args = (spec, edge_band, matrix)
    *two, sums = edge((1,), False, False, keep, second_pair, *shared_args, sums)
    *one, sums = edge((0,), False, True, keep, first_pair, lasts, *shared_args, sums)
    args = (keep, first_pair, second_pair, corners, lasts, *shared_args, sums)
    edge_one, one_squares, edge_two, two_squares, shared = edge((0, 1), True, True, *args, *one, *two)

    shared = lax.all_to_all(shared, "strip", 0, 0, tiled=True)
    (shared,) = call(
        functools.partial(clip_kernel, pixels),
        [VMEM] * 5,
        [((strips, width), f32)],
        [VMEM((width, LANES), f32), VMEM((slots, 8, LANES), f32)],
        10**8,
    )(shared, spec_squares, middle_squares, one_squares, two_squares)
    shared = lax.all_to_all(shared, "strip", 0, 0, tiled=True)
    (out,) = call(
        functools.partial(ratio_kernel, pixels),
        [VMEM] * 6,
        [((chan_count, n_rows, n_cols), bf16)],
        [VMEM((width, LANES), f32), VMEM((chan_count, n_rows, n_cols), bf16), dma((4,))],
        10**8,
        HBM,
    )(keep, shared, spec_exact, middle, edge_one, edge_two)
    return out


def solution(mesh):
    in_specs = (P("chan", "strip", "groups"), P("chan"))
    out_specs = P("chan", "strip", "groups")
    return jax.shard_map(shards, mesh=mesh, in_specs=in_specs, out_specs=out_specs, check_vma=False)
```
